32 devices in a mesh: node: 4 (over z), cls: 4 (over x, core), row: 2 (over y).
Axes of the slice: x: 2, y: 2, z: 4, core: 2. Of those that a mesh axis runs over, the one named last changes fastest.
Arguments:
- features: bfloat16 [128, 16384], P('row', 'node'), may hold values from -1 to 1
- class_weight: bfloat16 [128, 172], P('row', 'cls'), may hold values from -0.3984375 to 0.3984375
- class_bias: float32 [172], P('cls'), may hold values from -2 to 2
- part_position: int32 [16384], P(('node', 'row')), may hold values from 0 to 16383, as said below
- labels: int32 [16384], P(('node', 'row')), may hold values from 0 to 171
- train_mask: int32 [16384], P(('node', 'row')), may hold values 0 or 1
- export_rows: int32 [8, 128], P(('node', 'row')), may hold values from 0 to 2047, as said below
- tile_coords: int32 [8, 2, 128], P(('node', 'row')), may hold values from 0 to 23, as said below
- tile_count: int32 [8], P(('node', 'row')), may hold values from 16 to 128, as said below
- adjacency: bfloat16 [8, 128, 128, 128], P(('node', 'row'))
- corr_gain: float32 [172], P('cls'), may hold values from 0.3 to 1.5
Outputs:
- blended: float32 [172, 16384], P('cls', ('node', 'row'))
The draws below stay inside these ranges and needn't reach their ends.
Inputs may be any that keep to these rules, and one draw needn't show every extreme that they name: A permutation: node t of the training order stands at part position part_position[t]. Of the 2048 training positions of one index of node+row, at most 512 land in one block of 2048 part positions, and exactly 512 in some block, for every index. `export_rows`: 128 distinct row numbers of each part. `tile_coords`: row tiles lie in 0 to 15, column tiles in 0 to 23; the live slots of a part hold distinct pairs. `tile_count`: some part has all 128 slots live.
All inputs are finite; a program needn't handle non-finite values. No bound on the sum of `train_mask` on one device may be relied on, other than what follows from the above.
Results may differ from the reference program's by a relative error of at most 0.0044.
Values may be sent and summed in bfloat16 or wider, within the bound.
No kernel may reach another device: no remote copies, remote signals or barrier semaphores. Data moves between devices by JAX's collectives and lax.ppermute only.
A program may use at most 64 MiB of HBM per device.

```python
import math
import jax
import jax.numpy as jnp
from jax import lax

F = 128
C = 172
TILE = 128
ROWS = 2048
BOUNDARY = 128
NTMAX = 128
HOPS = 2
NPART = 8
NODES = 16384
N_ROW = 2


def shuffled(subkey):
    return jax.random.permutation(subkey, ROWS).astype(jnp.int32)


def relayout_tables(key):
    base_key = jax.random.fold_in(key, 101)
    key_sigma, key_slots, key_rows = jax.random.split(base_key, 3)
    even_share = ROWS // NPART
    sigma_order = jax.random.permutation(key_sigma, NPART).astype(jnp.int32)
    following = jnp.roll(sigma_order, -1)
    blocks_iota = jnp.arange(NPART, dtype=jnp.int32)
    raised = (blocks_iota[None, :] == sigma_order[:, None]).astype(jnp.int32)
    lowered = (blocks_iota[None, :] == following[:, None]).astype(jnp.int32)
    counts = even_share + even_share * (raised - lowered)
    bounds = jnp.cumsum(counts, axis=1)
    row_iota = jnp.arange(ROWS, dtype=jnp.int32)
    target_block = jnp.sum((bounds[:, None, :] <= row_iota[None, :, None]).astype(jnp.int32), axis=2)
    group_start = jnp.take_along_axis(bounds - counts, target_block, axis=1)
    rank_within = row_iota[None, :] - group_start
    offsets = jnp.cumsum(counts, axis=0) - counts
    slot_number = jnp.take_along_axis(offsets, target_block, axis=1) + rank_within
    slot_shuffle = jax.vmap(shuffled)(jax.random.split(key_slots, NPART))
    target = target_block * ROWS + slot_shuffle[target_block, slot_number]
    row_shuffle = jax.vmap(shuffled)(jax.random.split(key_rows, NPART))
    train_index = blocks_iota[:, None] * ROWS + row_shuffle
    part_position = jnp.zeros((NODES,), jnp.int32).at[train_index.reshape(-1)].set(target.reshape(-1).astype(jnp.int32))
    return part_position


def draw_part_position(key, part):
    return relayout_tables(key)


def draw_labels(key, part):
    base_key = jax.random.fold_in(key, 505)
    key_favoured, key_pick, key_home, key_other = jax.random.split(base_key, 4)
    group_count = NODES // TILE
    favoured = jax.random.randint(key_favoured, (group_count, 3), 0, C).astype(jnp.int32)
    pick = jax.random.randint(key_pick, (NODES,), 0, 3).astype(jnp.int32)
    at_home = jax.random.randint(key_home, (NODES,), 0, 5) < 4
    other = jax.random.randint(key_other, (NODES,), 0, C).astype(jnp.int32)
    group = jnp.arange(NODES, dtype=jnp.int32) // TILE
    chosen = favoured[group, pick]
    return jnp.where(at_home, chosen, other).astype(jnp.int32)


def tile_layout(key):
    base_key = jax.random.fold_in(key, 202)
    key_cells, key_load, key_full = jax.random.split(base_key, 3)
    row_tiles = ROWS // TILE
    column_tiles = (ROWS + NPART * BOUNDARY) // TILE
    cell_total = row_tiles * column_tiles

    def arrange(subkey):
        shuffled_cells = jax.random.permutation(subkey, cell_total).astype(jnp.int32)
        off_diagonal = (shuffled_cells % column_tiles != shuffled_cells // column_tiles).astype(jnp.int32)
        ordering = jnp.argsort(off_diagonal, stable=True)
        chosen = shuffled_cells[ordering][:NTMAX]
        return jnp.stack([chosen // column_tiles, chosen % column_tiles])
    placement = jax.vmap(arrange)(jax.random.split(key_cells, NPART))
    levels = 16
    load_level = jax.random.randint(key_load, (NPART,), 0, levels + 1)
    fullest = jax.random.randint(key_full, (), 0, NPART)
    load_level = jnp.where(jnp.arange(NPART, dtype=jnp.int32) == fullest, levels, load_level)
    live_count = row_tiles + (NTMAX - row_tiles) * load_level * load_level // (levels * levels)
    return (placement.astype(jnp.int32), live_count.astype(jnp.int32))


def draw_tile_coords(key, part):
    return tile_layout(key)[0]


def draw_tile_count(key, part):
    return tile_layout(key)[1]


def draw_export_rows(key, part):
    base_key = jax.random.fold_in(key, 303)

    def pick_rows(subkey):
        return jax.random.permutation(subkey, ROWS)[:BOUNDARY].astype(jnp.int32)
    return jax.vmap(pick_rows)(jax.random.split(base_key, NPART))


def draw_adjacency(key, part):
    base_key = jax.random.fold_in(key, 404)
    key_present, key_weight = jax.random.split(base_key, 2)
    array_shape = (NPART, NTMAX, TILE, TILE)
    per_row = TILE * NTMAX / (ROWS // TILE)
    degree = 30.0
    strength = jax.random.uniform(key_weight, array_shape, minval=0.5, maxval=1.5)
    presence_rate = min(degree / per_row, 0.5)
    present = (jax.random.uniform(key_present, array_shape) < presence_rate).astype(jnp.float32)
    factor = 1.0 / (presence_rate * per_row)
    return (present * strength * factor).astype(jnp.bfloat16)


def with_ends(values, key, smallest, top_value):
    dims = values.shape
    index_at = [jax.random.randint(jax.random.fold_in(key, axis), (), 0, dims[axis]) for axis in range(len(dims))]
    values = values.at[tuple(index_at)].set(smallest)
    longest = dims.index(max(dims))
    index_at[longest] = (index_at[longest] + 1) % dims[longest]
    return values.at[tuple(index_at)].set(top_value)


def level_of(key, shape, cuts, smallest, largest):
    loudness, own = 1.0, jax.random.fold_in(key, 6)
    for position, blocks in cuts:
        draws = jnp.exp(jax.random.uniform(jax.random.fold_in(own, position), (blocks,), jnp.float32, smallest / len(cuts), largest / len(cuts)))
        loudness = loudness * jnp.repeat(draws, shape[position] // blocks).reshape([-1 if axis == position else 1 for axis in range(len(shape))])
    return loudness


def setup_inputs(seed: int = 0) -> dict:
    seeds = jax.random.split(jax.random.key(seed), 12)
    features = jnp.clip(jax.random.uniform(seeds[0], (F, NODES), jnp.float32, -1.0, 1.0) * level_of(seeds[0], (F, NODES), ((0, 2), (1, 4)), -0.4, 0.0), -1.0, 1.0).astype(jnp.bfloat16)
    class_weight = jnp.clip(jax.random.uniform(seeds[1], (F, C), jnp.float32, -0.3984375, 0.3984375) * level_of(seeds[1], (F, C), ((0, 2), (1, 4)), -0.4, 0.0), -0.3984375, 0.3984375).astype(jnp.bfloat16)
    class_bias = jnp.clip(jax.random.uniform(seeds[2], (C,), jnp.float32, -2.0, 2.0) * level_of(seeds[2], (C,), ((0, 4),), -0.4, 0.0), -2.0, 2.0)
    part_position = draw_part_position(jax.random.fold_in(seeds[11], 71), 0)
    labels = draw_labels(jax.random.fold_in(seeds[11], 71), 0)
    train_mask = with_ends((jax.random.randint(seeds[5], (NODES,), 0, 4) < 1).astype(jnp.int32), jax.random.fold_in(seeds[5], 1), 0, 1)
    export_rows = draw_export_rows(jax.random.fold_in(seeds[11], 71), 0)
    tile_coords = draw_tile_coords(jax.random.fold_in(seeds[11], 71), 0)
    tile_count = draw_tile_count(jax.random.fold_in(seeds[11], 71), 0)
    adjacency = draw_adjacency(jax.random.fold_in(seeds[11], 71), 0)
    corr_gain = jnp.clip(jnp.exp(math.log(1.5) - 1.60943787 * jax.random.uniform(seeds[10], (C,), jnp.float32) ** level_of(seeds[10], (C,), ((0, 4),), -0.2, 0.2)), 0.3, 1.5)
    return dict(features=features, class_weight=class_weight, class_bias=class_bias, part_position=part_position, labels=labels, train_mask=train_mask, export_rows=export_rows, tile_coords=tile_coords, tile_count=tile_count, adjacency=adjacency, corr_gain=corr_gain)


alpha_mix = 0.8
spread_eps = 1e-06

def propagate(moved, export_rows, tile_coords, tile_count, adjacency):
    blocks = moved.reshape(C, NPART, ROWS)
    export_index = jnp.broadcast_to(export_rows[None, :, :], (C, NPART, BOUNDARY))
    exported = jnp.take_along_axis(blocks, export_index, axis=2).reshape(C, NPART * BOUNDARY)
    row_tiles = ROWS // TILE
    column_tiles = (ROWS + NPART * BOUNDARY) // TILE

    def one_part(part_index):
        local_rows = lax.dynamic_index_in_dim(blocks, part_index, 1, keepdims=False)
        source = jnp.concatenate([local_rows, exported], axis=1).reshape(C, column_tiles, TILE)
        tile_place = lax.dynamic_index_in_dim(tile_coords, part_index, 0, keepdims=False)
        tile_values = lax.dynamic_index_in_dim(adjacency, part_index, 0, keepdims=False)
        live_count = lax.dynamic_index_in_dim(tile_count, part_index, 0, keepdims=False)
        picked = jnp.take(source, tile_place[1], axis=1)
        product = jnp.einsum('ctb,tab->cta', picked.astype(jnp.float32), tile_values.astype(jnp.float32))
        live_mask = (jnp.arange(NTMAX, dtype=jnp.int32) < live_count).astype(jnp.float32)
        placing = (tile_place[0][:, None] == jnp.arange(row_tiles, dtype=jnp.int32)[None, :]).astype(jnp.float32)
        placing = placing * live_mask[:, None]
        spread_rows = jnp.einsum('cta,tr->cra', product, placing, precision=lax.Precision.HIGHEST)
        return spread_rows.reshape(C, ROWS)
    per_part = lax.map(one_part, jnp.arange(NPART, dtype=jnp.int32))
    return jnp.transpose(per_part, (1, 0, 2)).reshape(C, NODES)

def reference(features, class_weight, class_bias, part_position, labels, train_mask, export_rows, tile_coords, tile_count, adjacency, corr_gain):
    slice_width = F // N_ROW
    summed = jnp.zeros((C, NODES), jnp.float32)
    for slice_index in range(N_ROW):
        slice_features = features[slice_index * slice_width:(slice_index + 1) * slice_width]
        slice_weight = class_weight[slice_index * slice_width:(slice_index + 1) * slice_width]
        partial_value = lax.dot_general(slice_weight, slice_features, (((0,), (0,)), ((), ())), preferred_element_type=jnp.float32)
        partial_value = partial_value.astype(jnp.bfloat16)
        summed = summed + lax.optimization_barrier(partial_value).astype(jnp.float32)
    train_logits = (summed + class_bias[:, None]).astype(jnp.bfloat16)
    logits = jnp.zeros((C, NODES), jnp.bfloat16).at[:, part_position].set(train_logits)
    raised = jnp.exp(logits.astype(jnp.float32))
    totals = lax.optimization_barrier(jnp.sum(raised, axis=0))
    base = raised / totals[None, :]
    classes = jnp.arange(C, dtype=jnp.int32)
    truth = (labels[None, :] == classes[:, None]).astype(jnp.float32)
    trained = train_mask.astype(jnp.float32)[None, :]
    start_residual = trained * (truth - base)
    residual = start_residual
    for hop_index in range(HOPS):
        moved = residual.astype(jnp.bfloat16)
        spread_out = propagate(moved, export_rows, tile_coords, tile_count, adjacency)
        residual = (1.0 - alpha_mix) * start_residual + alpha_mix * spread_out
    mean_square = lax.optimization_barrier(jnp.mean(residual * residual, axis=0))
    corrected = base + corr_gain[:, None] * residual * lax.rsqrt(mean_square + spread_eps)[None, :]
    return jnp.where(train_mask[None, :] == 1, truth, corrected)
```

```python
import jax
import jax.numpy as jnp
from jax import lax
from jax.experimental import pallas as pl
from jax.experimental.pallas import tpu as pltpu
from jax.sharding import PartitionSpec as P

HOPS = 2
TILE = 128
LO = 4

alpha_mix = 0.8
spread_eps = 1e-06

F32 = jnp.float32
BF16 = jnp.bfloat16
I32 = jnp.int32
VMEM = pl.BlockSpec(memory_space=pltpu.VMEM)
SMEM = pl.BlockSpec(memory_space=pltpu.SMEM)


def iota(shape, dim):
    return lax.broadcasted_iota(I32, shape, dim)


def call(kernel, outs, ins, scratch=(), mb=32, flops=0, nbytes=0, name=None):
    return pl.pallas_call(
        kernel,
        out_shape=outs,
        in_specs=ins,
        out_specs=jax.tree.map(lambda _: VMEM, outs),
        scratch_shapes=list(scratch),
        compiler_params=pltpu.CompilerParams(vmem_limit_bytes=mb << 20),
        cost_estimate=pl.CostEstimate(flops=flops, bytes_accessed=nbytes, transcendentals=0),
        name=name,
    )


def shape(dims, dtype):
    return jax.ShapeDtypeStruct(dims, dtype)


def up(value, step):
    return -(-value // step) * step


def partial_scores(features, class_weight, row, row_count, rows_here, padded):
    depth, classes = class_weight.shape

    def kernel(row_ref, f_ref, w_ref, *outs):
        w = w_ref[...].astype(F32)
        w = jnp.concatenate([w, jnp.zeros((depth, TILE - classes), F32)], axis=1)
        w = w.T[:padded].astype(BF16)
        for k in [*range(1, row_count), 0]:
            at = pl.multiple_of(lax.rem(row_ref[0] + k, row_count) * rows_here, TILE)
            f = f_ref[:, pl.ds(at, rows_here)]
            outs[k][...] = jnp.dot(w, f, preferred_element_type=F32).astype(BF16)

    out = shape((padded, rows_here), BF16)
    return call(kernel, [out] * row_count, [SMEM, VMEM, VMEM], name="partial_scores")(
        row, features, class_weight
    )


def slot_tables(positions, rows_here, part_count, capacity):
    tiles = rows_here // TILE
    share = capacity // LO
    columns = part_count * share

    def kernel(p_ref, aux_ref, hot_ref):
        pos = p_ref[...]
        block = pos // rows_here
        before = (iota((TILE, TILE), 0) < iota((TILE, TILE), 1)).astype(BF16)
        ones = jnp.ones((TILE, TILE), BF16)
        above = (iota((tiles, tiles), 1) < iota((tiles, tiles), 0)).astype(BF16)
        rank = jnp.zeros((tiles, TILE), F32)
        for d in range(part_count):
            member = block == d
            m = member.astype(F32).astype(BF16)
            inside = jnp.dot(m, before, preferred_element_type=F32)
            each = jnp.dot(m, ones, preferred_element_type=F32).astype(BF16)
            offset = jnp.dot(above, each, preferred_element_type=F32)
            rank = jnp.where(member, inside + offset, rank)
        rank = rank.astype(I32)
        low = rank // share
        column = block * share + (rank - low * share)
        aux_ref[0] = low
        aux_ref[1] = pos - block * rows_here
        turned = jnp.concatenate([column, jnp.zeros((TILE - tiles, TILE), I32)], axis=0)
        turned = turned.astype(F32).T.astype(I32)
        across = iota((TILE, columns), 1)
        for j in range(tiles):
            hot = jnp.where(across == turned[:, j : j + 1], 1.0, 0.0)
            hot_ref[j * TILE : (j + 1) * TILE, :] = hot.astype(BF16)

    outs = [shape((2, tiles, TILE), I32), shape((rows_here, columns), BF16)]
    return call(kernel, outs, [VMEM], name="slot_tables")(positions)


def compact_scores(partials, bias, aux, hot, classes, padded):
    count = len(partials)
    rows_here = partials[0].shape[1]
    tiles = rows_here // TILE
    columns = hot.shape[1]
    blocks = columns // TILE
    high = rows_here // LO

    def kernel(*refs):
        parts = refs[:count]
        b_ref, aux_ref, hot_ref, out_ref, x_ref = refs[count:]
        bias_column = b_ref[...]
        row = iota((padded, TILE), 0)
        for j in range(tiles):
            cols = slice(j * TILE, (j + 1) * TILE)
            total = parts[0][:, cols].astype(F32)
            for other in parts[1:]:
                total = total + other[:, cols].astype(F32)
            value = (total + bias_column).astype(BF16).astype(F32)
            low = aux_ref[0, j : j + 1, :]
            place = aux_ref[1, j : j + 1, :]
            q = place // high
            h = place - q * high
            value = jnp.where(row == classes, (q + 1).astype(F32), value)
            value = jnp.where(row == classes + 1, (h // 16).astype(F32), value)
            value = jnp.where(row == classes + 2, (h - h // 16 * 16).astype(F32), value)
            for l in range(LO):
                x_ref[l * padded : (l + 1) * padded, cols] = jnp.where(low == l, value, 0.0).astype(BF16)
        laid = jnp.dot(x_ref[...], hot_ref[...], preferred_element_type=F32).astype(BF16)
        for d in range(blocks):
            out_ref[d] = laid[:, d * TILE : (d + 1) * TILE]

    return call(
        kernel,
        shape((blocks, LO * padded, TILE), BF16),
        [VMEM] * (count + 3),
        [pltpu.VMEM((LO * padded, rows_here), BF16)],
        name="compact_scores",
    )(*partials, bias, aux, hot)


def place_scores(received, rows_here, classes, padded):
    blocks = received.shape[0]
    tiles = rows_here // TILE
    high = rows_here // LO
    chunks = blocks * LO

    def kernel(r_ref, raised_ref, total_ref, x_ref, hot_ref):
        width = LO * padded
        lane = iota((8, width), 1) - iota((8, width), 0) * padded - classes
        pick = jnp.where(lane == 0, float(high), jnp.where(lane == 1, 16.0, jnp.where(lane == 2, 1.0, 0.0)))
        pick = jnp.where(iota((8, width), 0) < LO, pick, 0.0).astype(BF16)
        codes = [
            jnp.dot(pick, r_ref[s], preferred_element_type=F32) - float(high) for s in range(blocks)
        ]
        rest = jnp.zeros((TILE - 8 * blocks, TILE), F32)
        turned = jnp.concatenate(codes + [rest], axis=0).T.astype(I32) & (high - 1)
        across = iota((TILE, high), 1)
        for s in range(blocks):
            code = codes[s].astype(I32)
            for l in range(LO):
                at = (s * LO + l) * TILE
                lane_at = s * 8 + l
                hot = jnp.where(across == turned[:, lane_at : lane_at + 1], 1.0, 0.0)
                hot_ref[at : at + TILE, :] = hot.astype(BF16)
                group = code[l : l + 1, :] // high
                group = jnp.where(code[l : l + 1, :] < 0, -1, group)
                value = r_ref[s, l * padded : (l + 1) * padded, :].astype(F32)
                for q in range(LO):
                    x_ref[q * padded : (q + 1) * padded, at : at + TILE] = jnp.where(
                        group == q, value, 0.0
                    ).astype(BF16)
        logits = jnp.dot(x_ref[...], hot_ref[...], preferred_element_type=F32)
        row = iota((padded, TILE), 0)
        for i in range(tiles):
            q, c = divmod(i, tiles // LO)
            part = logits[q * padded : (q + 1) * padded, c * TILE : (c + 1) * TILE]
            raised = jnp.where(row < classes, jnp.exp(part), 0.0)
            raised_ref[i] = raised
            total_ref[i : i + 1, :] = jnp.sum(raised, axis=0, keepdims=True)

    return call(
        kernel,
        [shape((tiles, padded, TILE), F32), shape((tiles, TILE), F32)],
        [VMEM],
        [pltpu.VMEM((LO * padded, chunks * TILE), BF16), pltpu.VMEM((chunks * TILE, high), BF16)],
        name="place_scores",
    )(received)


def exported_columns(moved_tiles, export_row, padded):
    source = jnp.concatenate(moved_tiles, axis=1)
    rows = source.shape[1]
    hot = jnp.where(iota((rows, TILE), 0) == export_row, 1.0, 0.0).astype(BF16)
    return jnp.dot(source, hot, preferred_element_type=F32).astype(BF16)


def start_residuals(raised, totals, labels, mask, exports, first_class, classes):
    tiles, padded, _ = raised.shape
    count = len(totals)

    def kernel(first_ref, raised_ref, *refs):
        total_refs = refs[:count]
        label_ref, mask_ref, export_ref, base_ref, start_ref, moved_ref, out_ref = refs[count:]
        total = total_refs[0][...]
        for other in total_refs[1:]:
            total = total + other[...]
        row = iota((padded, TILE), 0)
        ids = jnp.where(row < classes, row + first_ref[0], -1)
        moved = []
        for i in range(tiles):
            base = raised_ref[i] / total[i : i + 1, :]
            truth = jnp.where(ids == label_ref[i : i + 1, :], 1.0, 0.0)
            start = mask_ref[i : i + 1, :].astype(F32) * (truth - base)
            base_ref[i] = base
            start_ref[i] = start
            moved.append(start.astype(BF16))
            moved_ref[i] = moved[-1]
        out_ref[...] = exported_columns(moved, export_ref[...], padded)

    full = shape((tiles, padded, TILE), F32)
    outs = [full, full, shape((tiles, padded, TILE), BF16), shape((padded, TILE), BF16)]
    return call(kernel, outs, [SMEM] + [VMEM] * (count + 4), name="start_residuals")(
        first_class, raised, *totals, labels, mask, exports
    )


def pair_tables(coords, live, here, counts, row_tiles):
    node_count, row_count = counts
    slots = coords.shape[1]
    places = up(slots + row_tiles, 2 * TILE)

    def kernel(here_ref, live_ref, c_ref, out_ref):
        row = c_ref[0:1, :]
        column = c_ref[1:2, :]
        slot = iota((1, slots), 1)
        part = jnp.maximum(column - row_tiles, 0)
        part_node = part // row_count
        part_row = part - part_node * row_count
        node_step = lax.rem(here_ref[0] - part_node + node_count, node_count)
        row_step = lax.rem(here_ref[1] - part_row + row_count, row_count)
        source = jnp.where(
            column < row_tiles, column, row_tiles + node_step * row_count + row_step
        )
        member = (iota((row_tiles, slots), 0) == row) & (slot < live_ref[0])
        m = jnp.where(member, 1.0, 0.0).astype(BF16)
        before = (iota((slots, slots), 0) < iota((slots, slots), 1)).astype(BF16)
        rank = jnp.dot(m, before, preferred_element_type=F32)
        number = jnp.dot(m, jnp.ones((slots, slots), BF16), preferred_element_type=F32).astype(I32)
        pairs = ((number + 1) // 2).astype(F32).astype(BF16)
        above = (iota((row_tiles, row_tiles), 1) < iota((row_tiles, row_tiles), 0)).astype(BF16)
        first = jnp.dot(above, pairs, preferred_element_type=F32)
        place = jnp.sum(jnp.where(member, 2.0 * first + rank + 1.0, 0.0), axis=0, keepdims=True)
        place = place.astype(I32) - 1
        hot = jnp.where(iota((places, slots), 0) == place, 1.0, 0.0).astype(BF16)
        line = iota((8, slots), 0)
        values = jnp.where(
            line == 0, slot, jnp.where(line == 1, source + 1, jnp.where(line == 2, row, 0))
        )
        table = lax.dot_general(
            values.astype(F32).astype(BF16), hot, (((1,), (1,)), ((), ())), preferred_element_type=F32
        )
        out_ref[...] = table.astype(I32)

    return call(kernel, shape((8, places), I32), [SMEM, SMEM, VMEM], name="pair_tables")(
        here, live, coords
    )


def hop(table, moved, boundary, adjacency, start, exports, last):
    tiles, padded, _ = moved.shape
    slots = adjacency.shape[0]
    count = len(boundary)
    pair_total = (slots + tiles) // 2
    sources = tiles + sum(b.shape[0] for b in boundary)

    def kernel(*refs):
        t_ref, moved_ref = refs[:2]
        boundary_refs = refs[2 : 2 + count]
        a_ref, start_ref, export_ref, first_out, second_out, s_ref, acc_ref = refs[2 + count :]
        s_ref[0] = jnp.zeros((padded, TILE), BF16)
        for i in range(tiles):
            s_ref[1 + i] = moved_ref[i]
        at = 1 + tiles
        for ref in boundary_refs:
            for k in range(ref.shape[0]):
                s_ref[at] = ref[k]
                at += 1
        acc_ref[...] = jnp.zeros_like(acc_ref)

        def step(k, carry):
            left = jnp.concatenate([s_ref[t_ref[1, 2 * k]], s_ref[t_ref[1, 2 * k + 1]]], axis=1)
            right = jnp.concatenate([a_ref[t_ref[0, 2 * k]], a_ref[t_ref[0, 2 * k + 1]]], axis=1)
            acc_ref[t_ref[2, 2 * k]] += lax.dot_general(
                left, right, (((1,), (1,)), ((), ())), preferred_element_type=F32
            )
            return carry

        lax.fori_loop(0, pair_total, step, 0, unroll=24)
        moved_out = []
        for i in range(tiles):
            residual = (1.0 - alpha_mix) * start_ref[i] + alpha_mix * acc_ref[i]
            if last:
                first_out[i] = residual
                second_out[i : i + 1, :] = jnp.sum(residual * residual, axis=0, keepdims=True)
            else:
                moved_out.append(residual.astype(BF16))
                first_out[i] = moved_out[-1]
        if not last:
            second_out[...] = exported_columns(moved_out, export_ref[...], padded)

    if last:
        outs = [shape((tiles, padded, TILE), F32), shape((tiles, TILE), F32)]
    else:
        outs = [shape((tiles, padded, TILE), BF16), shape((padded, TILE), BF16)]
    return call(
        kernel,
        outs,
        [SMEM] + [VMEM] * (count + 4),
        [pltpu.VMEM((1 + sources, padded, TILE), BF16), pltpu.VMEM((tiles, padded, TILE), F32)],
        name="hop",
    )(table, moved, *boundary, adjacency, start, exports)


def blend(base, residual, squares, labels, mask, gain, first_class, classes, class_total):
    tiles, padded, _ = base.shape
    count = len(squares)

    def kernel(first_ref, base_ref, residual_ref, *refs):
        square_refs = refs[:count]
        label_ref, mask_ref, gain_ref, out_ref = refs[count:]
        total = square_refs[0][...]
        for other in square_refs[1:]:
            total = total + other[...]
        inverse = lax.rsqrt(total / float(class_total) + spread_eps)
        ids = iota((padded, TILE), 0) + first_ref[0]
        for i in range(tiles):
            truth = jnp.where(ids == label_ref[i : i + 1, :], 1.0, 0.0)
            corrected = base_ref[i] + gain_ref[...] * residual_ref[i] * inverse[i : i + 1, :]
            blended = jnp.where(mask_ref[i : i + 1, :] == 1, truth, corrected)
            out_ref[:, i * TILE : (i + 1) * TILE] = blended[:classes]

    return call(
        kernel, shape((classes, tiles * TILE), F32), [SMEM] + [VMEM] * (count + 5), name="blend"
    )(first_class, base, residual, *squares, labels, mask, gain)


def shifted(value, axis, count, step):
    return lax.ppermute(value, axis, [(i, (i + step) % count) for i in range(count)])


def from_all(value, axis):
    count = lax.axis_size(axis)
    return [value] + [shifted(value, axis, count, step) for step in range(1, count)]


def gather_exports(value):
    group = jnp.stack(from_all(value, "row"))
    return from_all(group, "node")


def shards(
    features,
    class_weight,
    class_bias,
    part_position,
    labels,
    train_mask,
    export_rows,
    tile_coords,
    tile_count,
    adjacency,
    corr_gain,
):
    node_count = lax.axis_size("node")
    row_count = lax.axis_size("row")
    part_count = node_count * row_count
    rows_here = part_position.shape[0]
    classes = class_bias.shape[0]
    class_total = classes * lax.axis_size("cls")
    padded = up(classes + 3, 16)
    tiles = rows_here // TILE
    capacity = 2 * rows_here // part_count
    row = lax.axis_index("row").astype(I32)
    node = lax.axis_index("node").astype(I32)
    first_class = (lax.axis_index("cls") * classes).astype(I32)[None]
    tail = padded - classes
    bias = jnp.pad(class_bias, (0, tail))[:, None]
    gain = jnp.pad(corr_gain, (0, tail))[:, None]
    labels = labels.reshape(tiles, TILE)
    mask = train_mask.reshape(tiles, TILE)

    parts = partial_scores(features, class_weight, row[None], row_count, rows_here, padded)
    partials = [parts[0]] + [
        shifted(parts[step], "row", row_count, step) for step in range(1, row_count)
    ]
    aux, hot = slot_tables(part_position.reshape(tiles, TILE), rows_here, part_count, capacity)
    table = pair_tables(
        tile_coords[0], tile_count, jnp.stack([node, row]), (node_count, row_count), tiles
    )
    sending = compact_scores(partials, bias, aux, hot, classes, padded)
    blocks, width, _ = sending.shape
    share = capacity // LO
    if share != TILE:
        sending = sending.reshape(blocks, width, TILE // share, share).transpose(0, 2, 1, 3)
        sending = sending.reshape(part_count, width, share)
    received = lax.all_to_all(sending, ("node", "row"), split_axis=0, concat_axis=0, tiled=True)
    if share != TILE:
        received = received.reshape(blocks, TILE // share, width, share).transpose(0, 2, 1, 3)
        received = received.reshape(blocks, width, TILE)
    raised, total = place_scores(received, rows_here, classes, padded)
    totals = from_all(total, "cls")
    base, start, moved, out = start_residuals(
        raised, totals, labels, mask, export_rows, first_class, classes
    )
    for index in range(HOPS):
        boundary = gather_exports(out)
        moved, out = hop(
            table, moved, boundary, adjacency[0], start, export_rows, index == HOPS - 1
        )
    squares = from_all(out, "cls")
    return blend(
        base, moved, squares, labels, mask, gain, first_class, classes, class_total
    )


def solution(mesh):
    in_specs = (
        P("row", "node"),
        P("row", "cls"),
        P("cls"),
        P(("node", "row")),
        P(("node", "row")),
        P(("node", "row")),
        P(("node", "row"), None),
        P(("node", "row"), None, None),
        P(("node", "row")),
        P(("node", "row"), None, None, None),
        P("cls"),
    )
    out_specs = P("cls", ("node", "row"))
    return jax.shard_map(shards, mesh=mesh, in_specs=in_specs, out_specs=out_specs, check_vma=False)
```

```python
import jax
import jax.numpy as jnp
from jax import lax
from jax.experimental import pallas as pl
from jax.experimental.pallas import tpu as pltpu
from jax.sharding import PartitionSpec as P

HOPS = 2
TILE = 128
LO = 4
GROUP = 16
REST = 4

alpha_mix = 0.8
spread_eps = 1e-06

F32 = jnp.float32
BF16 = jnp.bfloat16
I32 = jnp.int32
VMEM = pl.BlockSpec(memory_space=pltpu.VMEM)
HBM = pl.BlockSpec(memory_space=pltpu.HBM)
SMEM = pl.BlockSpec(memory_space=pltpu.SMEM)


def iota(shape, dim):
    return lax.broadcasted_iota(I32, shape, dim)


def call(kernel, outs, ins, scratch=(), mb=12, flops=0, nbytes=0, name=None):
    return pl.pallas_call(
        kernel,
        out_shape=outs,
        in_specs=ins,
        out_specs=jax.tree.map(lambda _: VMEM, outs),
        scratch_shapes=list(scratch),
        compiler_params=pltpu.CompilerParams(vmem_limit_bytes=mb << 20),
        cost_estimate=pl.CostEstimate(flops=flops, bytes_accessed=nbytes, transcendentals=0),
        name=name,
    )


def in_hbm(*arrays):
    return [pltpu.with_memory_space_constraint(x, pltpu.HBM) for x in arrays]


def shape(dims, dtype):
    return jax.ShapeDtypeStruct(dims, dtype)


def up(value, step):
    return -(-value // step) * step


def padded_weight(weight, padded):
    classes, depth = weight.shape
    weight = weight.astype(F32)
    return jnp.concatenate([weight, jnp.zeros((padded - classes, depth), F32)], axis=0).astype(BF16)


def node_block(ref, here, step, row_count, rows_here):
    at = lax.rem(here[1] + step, row_count) * rows_here
    return ref.at[:, pl.ds(pl.multiple_of(at, TILE), rows_here)]


def partial_scores(features, weight, here, row_count, rows_here, padded):
    classes, depth = weight.shape
    steps = range(1, row_count)

    def kernel(here_ref, f_hbm, w_hbm, *refs):
        outs = refs[: row_count - 1]
        f_ref, w_ref, sems = refs[row_count - 1 :]
        copies = [pltpu.make_async_copy(w_hbm, w_ref, sems.at[0])]
        for step in steps:
            source = node_block(f_hbm, here_ref, step, row_count, rows_here)
            copies.append(pltpu.make_async_copy(source, f_ref.at[step - 1], sems.at[step]))
        for copy in copies:
            copy.start()
        copies[0].wait()
        w = padded_weight(w_ref[...], padded)
        for step in steps:
            copies[step].wait()
            score = jnp.dot(w, f_ref[step - 1], preferred_element_type=F32)
            outs[step - 1][...] = score.astype(BF16)

    out = shape((padded, rows_here), BF16)
    scratch = [
        pltpu.VMEM((row_count - 1, depth, rows_here), BF16),
        pltpu.VMEM((classes, depth), BF16),
        pltpu.SemaphoreType.DMA((row_count,)),
    ]
    return call(
        kernel, [out] * (row_count - 1), [SMEM, HBM, HBM], scratch, name="partial_scores"
    )(here, *in_hbm(features, weight))


def slot_tables(pos, me, rows_here, part_count, capacity, aux_ref, hot_ref):
    tiles = rows_here // TILE
    share = capacity // LO
    columns = part_count * share
    block = pos // rows_here
    before = (iota((TILE, TILE), 0) < iota((TILE, TILE), 1)).astype(BF16)
    ones = jnp.ones((TILE, TILE), BF16)
    above = (iota((tiles, tiles), 1) < iota((tiles, tiles), 0)).astype(BF16)
    rank = jnp.zeros((tiles, TILE), F32)
    for d in range(part_count):
        member = block == d
        m = member.astype(F32).astype(BF16)
        inside = jnp.dot(m, before, preferred_element_type=F32)
        each = jnp.dot(m, ones, preferred_element_type=F32).astype(BF16)
        offset = jnp.dot(above, each, preferred_element_type=F32)
        rank = jnp.where(member, inside + offset, rank)
    rank = rank.astype(I32)
    low = rank // share
    step = block - me
    step = jnp.where(step < 0, step + part_count, step)
    column = step * share + (rank - low * share)
    aux_ref[0] = low
    aux_ref[1] = pos - block * rows_here
    turned = jnp.concatenate([column, jnp.zeros((TILE - tiles, TILE), I32)], axis=0)
    turned = turned.astype(F32).T.astype(I32)
    across = iota((TILE, columns), 1)
    for j in range(tiles):
        hot = jnp.where(across == turned[:, j : j + 1], 1.0, 0.0)
        hot_ref[j * TILE : (j + 1) * TILE, :] = hot.astype(BF16)


def pair_tables(coords, live, here, counts, row_tiles, table_ref):
    node_count, row_count = counts
    slots = coords.shape[1]
    places = up(slots + row_tiles, 2 * REST)
    row = coords[0:1, :]
    column = coords[1:2, :]
    slot = iota((1, slots), 1)
    part = jnp.maximum(column - row_tiles, 0)
    part_node = part // row_count
    part_row = part - part_node * row_count
    node_step = here[0] - part_node
    node_step = jnp.where(node_step < 0, node_step + node_count, node_step)
    row_step = here[1] - part_row
    row_step = jnp.where(row_step < 0, row_step + row_count, row_step)
    before = (iota((slots, slots), 0) < iota((slots, slots), 1)).astype(BF16)
    ones = jnp.ones((slots, slots), BF16)
    above = (iota((row_tiles, row_tiles), 1) < iota((row_tiles, row_tiles), 0)).astype(BF16)
    line = iota((8, slots), 0)
    lane = iota((8, places), 1)
    for kind in range(2):
        if kind == 0:
            source = column
            wanted = column < row_tiles
        else:
            source = node_step * row_count + row_step
            wanted = column >= row_tiles
        member = (iota((row_tiles, slots), 0) == row) & (slot < live) & wanted
        m = jnp.where(member, 1.0, 0.0).astype(BF16)
        rank = jnp.dot(m, before, preferred_element_type=F32)
        number = jnp.dot(m, ones, preferred_element_type=F32).astype(I32)
        pairs = ((number + 1) // 2).astype(F32)
        first = jnp.dot(above, pairs.astype(BF16), preferred_element_type=F32)
        place = jnp.sum(jnp.where(member, 2.0 * first + rank + 1.0, 0.0), axis=0, keepdims=True)
        place = place.astype(I32) - 1
        hot = jnp.where(iota((places, slots), 0) == place, 1.0, 0.0).astype(BF16)
        values = jnp.where(
            line == 0, slot, jnp.where(line == 1, source + 1, jnp.where(line == 2, row, 0))
        )
        table = lax.dot_general(
            values.astype(F32).astype(BF16), hot, (((1,), (1,)), ((), ())), preferred_element_type=F32
        )
        total = jnp.sum(pairs, axis=0, keepdims=True).astype(I32)[:, :1]
        groups = total // GROUP
        rest = (total - groups * GROUP + REST - 1) // REST
        sizes = jnp.where(lane == 0, groups, rest)
        table_ref[kind] = jnp.where(iota((8, places), 0) == 3, sizes, table.astype(I32))


def own_tables(features, weight, positions, coords, live, here, rest, counts, padded, capacity):
    node_count, row_count = counts
    classes, depth = weight.shape
    tiles = positions.shape[0]
    rows_here = tiles * TILE
    part_count = node_count * row_count
    columns = part_count * capacity // LO
    labels, mask, exports, bias, gain, adjacency = rest
    slots = adjacency.shape[0]

    def kernel(here_ref, live_ref, *refs):
        f_hbm, w_hbm, p_hbm, c_hbm, l_hbm, m_hbm, e_hbm, b_hbm, g_hbm, a_hbm = refs[:10]
        score_ref, aux_ref, hot_ref, table_ref, l_ref, m_ref, e_ref, b_out, g_out, a_ref = refs[10:20]
        f_ref, w_ref, p_ref, c_ref, b_ref, g_ref, sems = refs[20:]
        source = node_block(f_hbm, here_ref, 0, row_count, rows_here)
        pairs = [
            (p_hbm, p_ref),
            (c_hbm, c_ref),
            (b_hbm, b_ref),
            (g_hbm, g_ref),
            (w_hbm, w_ref),
            (source, f_ref),
            (l_hbm, l_ref),
            (m_hbm, m_ref),
            (e_hbm, e_ref),
            (a_hbm, a_ref),
        ]
        copies = [pltpu.make_async_copy(a, b, sems.at[i]) for i, (a, b) in enumerate(pairs)]
        for copy in copies:
            copy.start()
        for copy in copies[:4]:
            copy.wait()
        slot_tables(p_ref[...], here_ref[2], rows_here, part_count, capacity, aux_ref, hot_ref)
        pair_tables(c_ref[...], live_ref[0], here_ref, counts, tiles, table_ref)
        b_out[...] = jnp.broadcast_to(turned_column(b_ref[...], padded), (padded, TILE))
        g_out[...] = jnp.broadcast_to(turned_column(g_ref[...], padded), (padded, TILE))
        for copy in copies[4:]:
            copy.wait()
        w = padded_weight(w_ref[...], padded)
        score_ref[...] = jnp.dot(w, f_ref[...], preferred_element_type=F32).astype(BF16)

    like = [shape(x.shape, x.dtype) for x in rest]
    outs = [
        shape((padded, rows_here), BF16),
        shape((2, tiles, TILE), I32),
        shape((rows_here, columns), BF16),
        shape((2, 8, up(slots + tiles, 2 * REST)), I32),
        like[0],
        like[1],
        like[2],
        shape((padded, TILE), F32),
        shape((padded, TILE), F32),
        like[5],
    ]
    scratch = [
        pltpu.VMEM((depth, rows_here), BF16),
        pltpu.VMEM((classes, depth), BF16),
        pltpu.VMEM(positions.shape, I32),
        pltpu.VMEM(coords.shape, I32),
        pltpu.VMEM(bias.shape, F32),
        pltpu.VMEM(gain.shape, F32),
        pltpu.SemaphoreType.DMA((10,)),
    ]
    return call(kernel, outs, [SMEM, SMEM] + [HBM] * 10, scratch, name="own_tables")(
        here, live, *in_hbm(features, weight, positions, coords, *rest)
    )


def turned_column(row, padded):
    row = jnp.concatenate([row, jnp.zeros((1, TILE - row.shape[1]), F32)], axis=1)
    return jnp.broadcast_to(row, (8, TILE)).T[:padded, 0:1]


def compact_scores(partials, bias, aux, hot, classes, padded):
    count = len(partials)
    rows_here = partials[0].shape[1]
    tiles = rows_here // TILE
    columns = hot.shape[1]
    blocks = columns // TILE
    high = rows_here // LO

    def kernel(*refs):
        parts = refs[:count]
        b_ref, aux_ref, hot_ref = refs[count : count + 3]
        outs, x_ref = refs[count + 3 : -1], refs[-1]
        bias_column = b_ref[...]
        row = iota((padded, TILE), 0)
        for j in range(tiles):
            cols = slice(j * TILE, (j + 1) * TILE)
            total = parts[0][:, cols].astype(F32)
            for other in parts[1:]:
                total = total + other[:, cols].astype(F32)
            value = (total + bias_column).astype(BF16).astype(F32)
            low = aux_ref[0, j : j + 1, :]
            place = aux_ref[1, j : j + 1, :]
            q = place // high
            h = place - q * high
            value = jnp.where(row == classes, (q + 1).astype(F32), value)
            value = jnp.where(row == classes + 1, (h // 16).astype(F32), value)
            value = jnp.where(row == classes + 2, (h - h // 16 * 16).astype(F32), value)
            for l in range(LO):
                x_ref[l * padded : (l + 1) * padded, cols] = jnp.where(low == l, value, 0.0).astype(BF16)
        laid = jnp.dot(x_ref[...], hot_ref[...], preferred_element_type=F32).astype(BF16)
        for d in range(blocks):
            outs[d][...] = laid[:, d * TILE : (d + 1) * TILE]

    return call(
        kernel,
        [shape((LO * padded, TILE), BF16)] * blocks,
        [VMEM] * (count + 3),
        [pltpu.VMEM((LO * padded, rows_here), BF16)],
        name="compact_scores",
    )(*partials, bias, aux, hot)


def place_scores(received, rows_here, classes, padded):
    blocks = len(received)
    tiles = rows_here // TILE
    high = rows_here // LO
    chunks = blocks * LO

    def kernel(*refs):
        r_refs = refs[:blocks]
        raised_ref, total_ref, x_ref, hot_ref = refs[blocks:]
        width = LO * padded
        lane = iota((8, width), 1) - iota((8, width), 0) * padded - classes
        pick = jnp.where(lane == 0, float(high), jnp.where(lane == 1, 16.0, jnp.where(lane == 2, 1.0, 0.0)))
        pick = jnp.where(iota((8, width), 0) < LO, pick, 0.0).astype(BF16)
        codes = [
            jnp.dot(pick, r_refs[s][...], preferred_element_type=F32) - float(high) for s in range(blocks)
        ]
        rest = jnp.zeros((TILE - 8 * blocks, TILE), F32)
        turned = jnp.concatenate(codes + [rest], axis=0).T.astype(I32) & (high - 1)
        across = iota((TILE, high), 1)
        for s in range(blocks):
            code = codes[s].astype(I32)
            for l in range(LO):
                at = (s * LO + l) * TILE
                lane_at = s * 8 + l
                hot = jnp.where(across == turned[:, lane_at : lane_at + 1], 1.0, 0.0)
                hot_ref[at : at + TILE, :] = hot.astype(BF16)
                group = code[l : l + 1, :] // high
                group = jnp.where(code[l : l + 1, :] < 0, -1, group)
                value = r_refs[s][l * padded : (l + 1) * padded, :].astype(F32)
                for q in range(LO):
                    x_ref[q * padded : (q + 1) * padded, at : at + TILE] = jnp.where(
                        group == q, value, 0.0
                    ).astype(BF16)
        logits = jnp.dot(x_ref[...], hot_ref[...], preferred_element_type=F32)
        row = iota((padded, TILE), 0)
        for i in range(tiles):
            q, c = divmod(i, tiles // LO)
            part = logits[q * padded : (q + 1) * padded, c * TILE : (c + 1) * TILE]
            raised = jnp.where(row < classes, jnp.exp(part), 0.0)
            raised_ref[i] = raised
            total_ref[i : i + 1, :] = jnp.sum(raised, axis=0, keepdims=True)

    return call(
        kernel,
        [shape((tiles, padded, TILE), F32), shape((tiles, TILE), F32)],
        [VMEM] * blocks,
        [pltpu.VMEM((LO * padded, chunks * TILE), BF16), pltpu.VMEM((chunks * TILE, high), BF16)],
        name="place_scores",
    )(*received)


def exported_columns(moved_tiles, export_row, padded):
    source = jnp.concatenate(moved_tiles, axis=1)
    rows = source.shape[1]
    hot = jnp.where(iota((rows, TILE), 0) == export_row, 1.0, 0.0).astype(BF16)
    return jnp.dot(source, hot, preferred_element_type=F32).astype(BF16)


def start_residuals(raised, totals, labels, mask, exports, here, classes):
    tiles, padded, _ = raised.shape
    count = len(totals)

    def kernel(here_ref, raised_ref, *refs):
        total_refs = refs[:count]
        label_ref, mask_ref, export_ref, base_ref, start_ref, moved_ref, out_ref = refs[count:]
        total = total_refs[0][...]
        for other in total_refs[1:]:
            total = total + other[...]
        row = iota((padded, TILE), 0)
        ids = jnp.where(row < classes, row + here_ref[3], -1)
        moved = []
        for i in range(tiles):
            base = raised_ref[i] / total[i : i + 1, :]
            truth = jnp.where(ids == label_ref[i : i + 1, :], 1.0, 0.0)
            start = mask_ref[i : i + 1, :].astype(F32) * (truth - base)
            base_ref[i] = base
            start_ref[i] = start
            moved.append(start.astype(BF16))
            moved_ref[i] = moved[-1]
        out_ref[...] = exported_columns(moved, export_ref[...], padded)

    full = shape((tiles, padded, TILE), F32)
    outs = [full, full, shape((tiles, padded, TILE), BF16), shape((padded, TILE), BF16)]
    return call(kernel, outs, [SMEM] + [VMEM] * (count + 4), name="start_residuals")(
        here, raised, *totals, labels, mask, exports
    )


def pair_products(table_ref, kind, s_ref, a_ref, acc_ref):
    acc_ref[...] = jnp.zeros_like(acc_ref)

    def product(k):
        slots = [table_ref[kind, 0, k], table_ref[kind, 0, k + 1]]
        sources = [table_ref[kind, 1, k], table_ref[kind, 1, k + 1]]
        left = jnp.concatenate([s_ref[j] for j in sources], axis=1)
        right = jnp.concatenate([a_ref[t] for t in slots], axis=1)
        acc_ref[table_ref[kind, 2, k]] += lax.dot_general(
            left, right, (((1,), (1,)), ((), ())), preferred_element_type=F32
        )

    def several(first, count):
        def step(group, carry):
            for u in range(count):
                product(2 * (first + group * count + u))
            return carry

        return step

    groups = table_ref[kind, 3, 0]
    lax.fori_loop(0, groups, several(0, GROUP), 0)
    lax.fori_loop(0, table_ref[kind, 3, 1], several(groups * GROUP, REST), 0)


def own_products(table, moved, adjacency):
    tiles, padded, _ = moved.shape

    def kernel(t_ref, moved_ref, a_ref, acc_ref, s_ref):
        s_ref[0] = jnp.zeros((padded, TILE), BF16)
        for i in range(tiles):
            s_ref[1 + i] = moved_ref[i]
        pair_products(t_ref, 0, s_ref, a_ref, acc_ref)

    return call(
        kernel,
        shape((tiles, padded, TILE), F32),
        [SMEM, VMEM, VMEM],
        [pltpu.VMEM((1 + tiles, padded, TILE), BF16)],
        name="own_products",
    )(table, moved, adjacency)


def hop(table, boundary, adjacency, own, start, exports, last):
    tiles, padded, _ = start.shape
    count = len(boundary)
    sources = sum(b.shape[0] for b in boundary)

    def kernel(*refs):
        t_ref = refs[0]
        boundary_refs = refs[1 : 1 + count]
        a_ref, own_ref, start_ref, export_ref, first_out, second_out, s_ref, acc_ref = refs[1 + count :]
        s_ref[0] = jnp.zeros((padded, TILE), BF16)
        at = 1
        for ref in boundary_refs:
            for k in range(ref.shape[0]):
                s_ref[at] = ref[k]
                at += 1
        pair_products(t_ref, 1, s_ref, a_ref, acc_ref)
        moved_out = []
        for i in range(tiles):
            spread = own_ref[i] + acc_ref[i]
            residual = (1.0 - alpha_mix) * start_ref[i] + alpha_mix * spread
            if last:
                first_out[i] = residual
                second_out[i : i + 1, :] = jnp.sum(residual * residual, axis=0, keepdims=True)
            else:
                moved_out.append(residual.astype(BF16))
                first_out[i] = moved_out[-1]
        if not last:
            second_out[...] = exported_columns(moved_out, export_ref[...], padded)

    if last:
        outs = [shape((tiles, padded, TILE), F32), shape((tiles, TILE), F32)]
    else:
        outs = [shape((tiles, padded, TILE), BF16), shape((padded, TILE), BF16)]
    return call(
        kernel,
        outs,
        [SMEM] + [VMEM] * (count + 4),
        [pltpu.VMEM((1 + sources, padded, TILE), BF16), pltpu.VMEM((tiles, padded, TILE), F32)],
        name="hop",
    )(table, *boundary, adjacency, own, start, exports)


def blend_terms(base, residual, labels, mask, gain, here):
    tiles, padded, _ = base.shape

    def kernel(here_ref, base_ref, residual_ref, label_ref, mask_ref, gain_ref, term_ref, factor_ref):
        ids = iota((padded, TILE), 0) + here_ref[3]
        gains = gain_ref[...]
        for i in range(tiles):
            truth = jnp.where(ids == label_ref[i : i + 1, :], 1.0, 0.0)
            trained = mask_ref[i : i + 1, :] == 1
            term_ref[i] = jnp.where(trained, truth, base_ref[i])
            factor_ref[i] = jnp.where(trained, 0.0, gains * residual_ref[i])

    full = shape((tiles, padded, TILE), F32)
    return call(kernel, [full, full], [SMEM] + [VMEM] * 5, name="blend_terms")(
        here, base, residual, labels, mask, gain
    )


def blend(term, factor, squares, classes, class_total):
    tiles, padded, _ = term.shape
    count = len(squares)

    def kernel(term_ref, factor_ref, *refs):
        square_refs = refs[:count]
        out_ref = refs[count]
        total = square_refs[0][...]
        for other in square_refs[1:]:
            total = total + other[...]
        inverse = lax.rsqrt(total / float(class_total) + spread_eps)
        for i in range(tiles):
            blended = term_ref[i] + factor_ref[i] * inverse[i : i + 1, :]
            out_ref[:, i * TILE : (i + 1) * TILE] = blended[:classes]

    return call(
        kernel, shape((classes, tiles * TILE), F32), [VMEM] * (count + 2), name="blend"
    )(term, factor, *squares)


def shifted(value, axis, count, step):
    return lax.ppermute(value, axis, [(i, (i + step) % count) for i in range(count)])


def from_all(value, axis):
    count = lax.axis_size(axis)
    return [value] + [shifted(value, axis, count, step) for step in range(1, count)]


def shards(
    features,
    class_weight,
    class_bias,
    part_position,
    labels,
    train_mask,
    export_rows,
    tile_coords,
    tile_count,
    adjacency,
    corr_gain,
):
    node_count = lax.axis_size("node")
    row_count = lax.axis_size("row")
    part_count = node_count * row_count
    rows_here = part_position.shape[0]
    classes = class_bias.shape[0]
    class_total = classes * lax.axis_size("cls")
    padded = up(classes + 3, 16)
    tiles = rows_here // TILE
    capacity = 2 * rows_here // part_count
    counts = (node_count, row_count)
    row = lax.axis_index("row").astype(I32)
    node = lax.axis_index("node").astype(I32)
    first_class = (lax.axis_index("cls") * classes).astype(I32)
    labels = labels.reshape(tiles, TILE)
    mask = train_mask.reshape(tiles, TILE)
    weight = class_weight.T
    share = capacity // LO
    direct = share == TILE
    me = node * row_count + row if direct else jnp.zeros((), I32)
    here = jnp.stack([node, row, me, first_class])

    parts = partial_scores(features, weight, here, row_count, rows_here, padded)
    partials = [
        shifted(parts[step - 1], "row", row_count, step) for step in range(1, row_count)
    ]
    rest = (labels, mask, export_rows, class_bias[None], corr_gain[None], adjacency[0])
    score, aux, hot, table, labels, mask, exports, bias, gain, adjacency = own_tables(
        features,
        weight,
        part_position.reshape(tiles, TILE),
        tile_coords[0],
        tile_count,
        here,
        rest,
        counts,
        padded,
        capacity,
    )
    sending = compact_scores([score] + partials, bias, aux, hot, classes, padded)
    if direct:
        received = [sending[0]] + [
            shifted(sending[step], ("node", "row"), part_count, step) for step in range(1, part_count)
        ]
    else:
        blocks, width = len(sending), sending[0].shape[0]
        sent = jnp.stack(sending).reshape(blocks, width, TILE // share, share).transpose(0, 2, 1, 3)
        sent = sent.reshape(part_count, width, share)
        got = lax.all_to_all(sent, ("node", "row"), split_axis=0, concat_axis=0, tiled=True)
        got = got.reshape(blocks, TILE // share, width, share).transpose(0, 2, 1, 3)
        got = got.reshape(blocks, width, TILE)
        received = [got[s] for s in range(blocks)]
    raised, total = place_scores(received, rows_here, classes, padded)
    totals = from_all(total, "cls")
    base, start, moved, out = start_residuals(
        raised, totals, labels, mask, exports, here, classes
    )
    for index in range(HOPS):
        group = jnp.stack(from_all(out, "row"))
        own = own_products(table, moved, adjacency)
        group, own = lax.optimization_barrier((group, own))
        boundary = from_all(group, "node")
        moved, out = hop(
            table, boundary, adjacency, own, start, exports, index == HOPS - 1
        )
    squares = from_all(out, "cls")
    term, factor = blend_terms(base, moved, labels, mask, gain, here)
    return blend(term, factor, squares, classes, class_total)


def solution(mesh):
    in_specs = (
        P("row", "node"),
        P("row", "cls"),
        P("cls"),
        P(("node", "row")),
        P(("node", "row")),
        P(("node", "row")),
        P(("node", "row"), None),
        P(("node", "row"), None, None),
        P(("node", "row")),
        P(("node", "row"), None, None, None),
        P("cls"),
    )
    out_specs = P("cls", ("node", "row"))
    return jax.shard_map(shards, mesh=mesh, in_specs=in_specs, out_specs=out_specs, check_vma=False)
```

```python
import jax
import jax.numpy as jnp
from jax import lax
from jax.experimental import pallas as pl
from jax.experimental.pallas import tpu as pltpu
from jax.sharding import PartitionSpec as P

HOPS = 2
TILE = 128
LO = 4
GROUP = 16
REST = 4
FIRST = 4

alpha_mix = 0.8
spread_eps = 1e-06

F32 = jnp.float32
BF16 = jnp.bfloat16
I32 = jnp.int32
VMEM = pl.BlockSpec(memory_space=pltpu.VMEM)
HBM = pl.BlockSpec(memory_space=pltpu.HBM)
SMEM = pl.BlockSpec(memory_space=pltpu.SMEM)


def iota(shape, dim):
    return lax.broadcasted_iota(I32, shape, dim)


def call(kernel, outs, ins, scratch=(), mb=12, flops=0, nbytes=0, name=None, where=None):
    return pl.pallas_call(
        kernel,
        out_shape=outs,
        in_specs=ins,
        out_specs=where or jax.tree.map(lambda _: VMEM, outs),
        scratch_shapes=list(scratch),
        compiler_params=pltpu.CompilerParams(vmem_limit_bytes=mb << 20),
        cost_estimate=pl.CostEstimate(flops=flops, bytes_accessed=nbytes, transcendentals=0),
        name=name,
    )


def in_hbm(*arrays):
    return [pltpu.with_memory_space_constraint(x, pltpu.HBM) for x in arrays]


def in_smem(x):
    return pltpu.with_memory_space_constraint(x, pltpu.SMEM)


def shape(dims, dtype):
    return jax.ShapeDtypeStruct(dims, dtype)


def up(value, step):
    return -(-value // step) * step


def step_between(a, b, count):
    assert count & (count - 1) == 0
    return a ^ b


def padded_weight(weight, padded):
    classes, depth = weight.shape
    weight = weight.astype(F32)
    return jnp.concatenate([weight, jnp.zeros((padded - classes, depth), F32)], axis=0).astype(BF16)


def node_block(ref, step, row_count, rows_here):
    at = step_between(lax.axis_index("row").astype(I32), step, row_count) * rows_here
    return ref.at[:, pl.ds(pl.multiple_of(at, TILE), rows_here)]


def partial_scores(features, weight, row_count, rows_here, padded):
    classes, depth = weight.shape
    steps = range(1, row_count)

    def kernel(f_hbm, w_hbm, *refs):
        outs = refs[: row_count - 1]
        f_ref, w_ref, sems = refs[row_count - 1 :]
        copies = [pltpu.make_async_copy(w_hbm, w_ref, sems.at[0])]
        for step in steps:
            source = node_block(f_hbm, step, row_count, rows_here)
            copies.append(pltpu.make_async_copy(source, f_ref.at[step - 1], sems.at[step]))
        for copy in copies:
            copy.start()
        copies[0].wait()
        w = padded_weight(w_ref[...], padded)
        for step in steps:
            copies[step].wait()
            score = jnp.dot(w, f_ref[step - 1], preferred_element_type=F32)
            outs[step - 1][...] = score.astype(BF16)

    out = shape((padded, rows_here), BF16)
    scratch = [
        pltpu.VMEM((row_count - 1, depth, rows_here), BF16),
        pltpu.VMEM((classes, depth), BF16),
        pltpu.SemaphoreType.DMA((row_count,)),
    ]
    return call(
        kernel, [out] * (row_count - 1), [HBM, HBM], scratch, name="partial_scores"
    )(*in_hbm(features, weight))


def slot_tables(pos, me, rows_here, part_count, capacity, aux_ref, hot_ref):
    tiles = rows_here // TILE
    share = capacity // LO
    columns = part_count * share
    block = pos // rows_here
    before = (iota((TILE, TILE), 0) < iota((TILE, TILE), 1)).astype(BF16)
    ones = jnp.ones((TILE, TILE), BF16)
    above = (iota((tiles, tiles), 1) < iota((tiles, tiles), 0)).astype(BF16)
    rank = jnp.zeros((tiles, TILE), F32)
    for d in range(part_count):
        member = block == d
        m = member.astype(F32).astype(BF16)
        inside = jnp.dot(m, before, preferred_element_type=F32)
        each = jnp.dot(m, ones, preferred_element_type=F32).astype(BF16)
        offset = jnp.dot(above, each, preferred_element_type=F32)
        rank = jnp.where(member, inside + offset, rank)
    rank = rank.astype(I32)
    low = rank // share
    column = step_between(block, me, part_count) * share + (rank - low * share)
    place = pos - block * rows_here
    power = place // TILE
    scale = jnp.ones((tiles, TILE), F32)
    for j in range(1, tiles):
        scale = jnp.where(power >= j, 2.0 * scale, scale)
    aux_ref[0] = low.astype(F32)
    aux_ref[1] = (place - power * TILE + TILE).astype(F32) * scale
    turned = jnp.concatenate([column, jnp.zeros((TILE - tiles, TILE), I32)], axis=0)
    turned = turned.astype(F32).T.astype(I32)
    across = iota((TILE, columns), 1)
    for j in range(tiles):
        hot = jnp.where(across == turned[:, j : j + 1], 1.0, 0.0)
        hot_ref[j * TILE : (j + 1) * TILE, :] = hot.astype(BF16)


def pair_tables(coords, live, here, counts, row_tiles, table_ref):
    node_count, row_count = counts
    slots = coords.shape[1]
    places = up(slots + row_tiles, 2 * REST)
    row = coords[0:1, :]
    column = coords[1:2, :]
    slot = iota((1, slots), 1)
    part = jnp.maximum(column - row_tiles, 0)
    part_node = part // row_count
    part_row = part - part_node * row_count
    node_step = step_between(part_node, here[0], node_count)
    row_step = step_between(part_row, here[1], row_count)
    before = (iota((slots, slots), 0) < iota((slots, slots), 1)).astype(BF16)
    ones = jnp.ones((slots, slots), BF16)
    above = (iota((row_tiles, row_tiles), 1) < iota((row_tiles, row_tiles), 0)).astype(BF16)
    line = iota((8, slots), 0)
    lane = iota((8, places), 1)
    for kind in range(2):
        if kind == 0:
            source = column
            wanted = column < row_tiles
        else:
            source = node_step * row_count + row_step
            wanted = column >= row_tiles
        member = (iota((row_tiles, slots), 0) == row) & (slot < live) & wanted
        m = jnp.where(member, 1.0, 0.0).astype(BF16)
        rank = jnp.dot(m, before, preferred_element_type=F32)
        number = jnp.dot(m, ones, preferred_element_type=F32).astype(I32)
        pairs = ((number + 1) // 2).astype(F32)
        first = jnp.dot(above, pairs.astype(BF16), preferred_element_type=F32)
        place = jnp.sum(jnp.where(member, 2.0 * first + rank + 1.0, 0.0), axis=0, keepdims=True)
        place = place.astype(I32) - 1
        hot = jnp.where(iota((places, slots), 0) == place, 1.0, 0.0).astype(BF16)
        values = jnp.where(
            line == 0, slot, jnp.where(line == 1, source + 1, jnp.where(line == 2, row, 0))
        )
        table = lax.dot_general(
            values.astype(F32).astype(BF16), hot, (((1,), (1,)), ((), ())), preferred_element_type=F32
        )
        total = jnp.sum(pairs, axis=0, keepdims=True).astype(I32)[:, :1]
        groups = total // GROUP
        rest = (total - groups * GROUP + REST - 1) // REST
        sizes = jnp.where(lane == 0, groups, rest)
        table_ref[kind] = jnp.where(iota((8, places), 0) == 3, sizes, table.astype(I32))


def own_tables(features, weight, positions, coords, live, rest, counts, padded, capacity, direct):
    node_count, row_count = counts
    classes, depth = weight.shape
    tiles = positions.shape[0]
    rows_here = tiles * TILE
    part_count = node_count * row_count
    columns = part_count * capacity // LO
    labels, mask, exports, bias, gain, adjacency = rest
    slots = adjacency.shape[0]

    def kernel(live_ref, *refs):
        node, row = lax.axis_index("node").astype(I32), lax.axis_index("row").astype(I32)
        f_hbm, w_hbm, p_hbm, c_hbm, l_hbm, m_hbm, e_hbm, b_hbm, g_hbm, a_hbm = refs[:10]
        score_ref, aux_ref, hot_ref, table_out, l_ref, m_ref, e_ref, b_out, g_out, a_ref, i_out = refs[10:21]
        f_ref, w_ref, p_ref, c_ref, b_ref, g_ref, t_ref, sems = refs[21:]
        source = node_block(f_hbm, 0, row_count, rows_here)
        pairs = [
            (p_hbm, p_ref),
            (c_hbm, c_ref),
            (b_hbm, b_ref),
            (g_hbm, g_ref),
            (w_hbm, w_ref),
            (source, f_ref),
            (l_hbm, l_ref),
            (m_hbm, m_ref),
            (e_hbm, e_ref),
            (a_hbm, a_ref),
        ]
        copies = [pltpu.make_async_copy(a, b, sems.at[i]) for i, (a, b) in enumerate(pairs)]
        for copy in copies:
            copy.start()
        for copy in copies[:4]:
            copy.wait()
        me = node * row_count + row if direct else 0
        slot_tables(p_ref[...], me, rows_here, part_count, capacity, aux_ref, hot_ref)
        pair_tables(c_ref[...], live_ref[0], (node, row), counts, tiles, t_ref)
        table_copy = pltpu.make_async_copy(t_ref, table_out, sems.at[10])
        table_copy.start()
        b_out[...] = jnp.broadcast_to(turned_column(b_ref[...], padded), (padded, TILE))
        g_out[...] = jnp.broadcast_to(turned_column(g_ref[...], padded), (padded, TILE))
        line = iota((padded, TILE), 0)
        first = lax.axis_index("cls").astype(I32) * classes
        i_out[...] = jnp.where(line < classes, line + first, -1)
        table_copy.wait()
        for copy in copies[4:]:
            copy.wait()
        w = padded_weight(w_ref[...], padded)
        score_ref[...] = jnp.dot(w, f_ref[...], preferred_element_type=F32).astype(BF16)

    like = [shape(x.shape, x.dtype) for x in rest]
    outs = [
        shape((padded, rows_here), BF16),
        shape((2, tiles, TILE), F32),
        shape((rows_here, columns), BF16),
        pltpu.SMEM((2, 8, up(slots + tiles, 2 * REST)), I32),
        like[0],
        like[1],
        like[2],
        shape((padded, TILE), F32),
        shape((padded, TILE), F32),
        like[5],
        shape((padded, TILE), I32),
    ]
    scratch = [
        pltpu.VMEM((depth, rows_here), BF16),
        pltpu.VMEM((classes, depth), BF16),
        pltpu.VMEM(positions.shape, I32),
        pltpu.VMEM(coords.shape, I32),
        pltpu.VMEM(bias.shape, F32),
        pltpu.VMEM(gain.shape, F32),
        pltpu.VMEM(outs[3].shape, I32),
        pltpu.SemaphoreType.DMA((11,)),
    ]
    where = [VMEM] * 3 + [SMEM] + [VMEM] * 7
    return call(kernel, outs, [SMEM] + [HBM] * 10, scratch, name="own_tables", where=where)(
        live, *in_hbm(features, weight, positions, coords, *rest)
    )


def turned_column(row, padded):
    row = jnp.concatenate([row, jnp.zeros((1, TILE - row.shape[1]), F32)], axis=1)
    return jnp.broadcast_to(row, (8, TILE)).T[:padded, 0:1]


def laid_block(laid, at, rows, padded):
    block = laid[:, at * TILE : (at + 1) * TILE]
    kept = jnp.concatenate([block[l * padded : l * padded + rows] for l in range(LO)], axis=0)
    return kept.astype(BF16)


def compact_scores(partials, bias, aux, hot, classes, padded):
    count = len(partials)
    rows_here = partials[0].shape[1]
    tiles = rows_here // TILE
    rows = classes + 1

    def kernel(*refs):
        parts = refs[:count]
        b_ref, aux_ref, hot_ref = refs[count : count + 3]
        outs, x_ref = refs[count + 3 : -1], refs[-1]
        bias_column = b_ref[...]
        row = iota((padded, TILE), 0)
        for j in range(tiles):
            cols = slice(j * TILE, (j + 1) * TILE)
            total = parts[0][:, cols].astype(F32)
            for other in parts[1:]:
                total = total + other[:, cols].astype(F32)
            value = (total + bias_column).astype(BF16).astype(F32)
            low = aux_ref[0, j : j + 1, :]
            value = jnp.where(row == classes, aux_ref[1, j : j + 1, :], value)
            for l in range(LO):
                x_ref[l * padded : (l + 1) * padded, cols] = jnp.where(low == l, value, 0.0).astype(BF16)
        laid = jnp.dot(x_ref[...], hot_ref[...], preferred_element_type=F32)
        for d, out in enumerate(outs):
            out[...] = laid_block(laid, d, rows, padded)

    return call(
        kernel,
        [shape((LO * rows, TILE), BF16)] * (hot.shape[1] // TILE),
        [VMEM] * (count + 3),
        [pltpu.VMEM((LO * padded, rows_here), BF16)],
        name="compact_scores",
    )(*partials, bias, aux, hot)


def placed(r_refs, x_ref, hot_ref, rows_here, classes, padded):
    rows = classes + 1
    high = rows_here // LO
    blocks = len(r_refs)
    width = LO * rows
    pick = iota((8, width), 1) - iota((8, width), 0) * rows == classes
    pick = jnp.where(pick & (iota((8, width), 0) < LO), 1.0, 0.0).astype(BF16)
    held = [jnp.dot(pick, ref[...], preferred_element_type=F32) for ref in r_refs]
    held = jnp.concatenate(held, axis=0)
    power = jnp.zeros(held.shape, I32)
    scale = jnp.ones(held.shape, F32)
    for j in range(1, rows_here // TILE):
        above = held >= float(TILE << j)
        power = jnp.where(above, j, power)
        scale = jnp.where(above, 0.5**j, scale)
    code = jnp.where(held > 0.0, power * TILE + (held * scale).astype(I32) - TILE, -1)
    group = jnp.where(code < 0, -1, code // high)
    inner = (code & (high - 1)).astype(F32)
    rest = jnp.zeros((TILE - 8 * blocks, TILE), F32)
    turned = jnp.concatenate([inner, rest], axis=0).T.astype(I32)
    across = iota((TILE, high), 1)
    tail = jnp.zeros((padded - rows, TILE), F32)
    for s in range(blocks):
        block = r_refs[s][...].astype(F32)
        for l in range(LO):
            at = (s * LO + l) * TILE
            lane = s * 8 + l
            hot = jnp.where(across == turned[:, lane : lane + 1], 1.0, 0.0)
            hot_ref[at : at + TILE, :] = hot.astype(BF16)
            value = jnp.concatenate([block[l * rows : (l + 1) * rows], tail], axis=0)
            mine = group[lane : lane + 1, :]
            for q in range(LO):
                x_ref[q * padded : (q + 1) * padded, at : at + TILE] = jnp.where(
                    mine == q, value, 0.0
                ).astype(BF16)
    return jnp.dot(x_ref[...], hot_ref[...], preferred_element_type=F32)


def place_scratch(blocks, rows_here, padded):
    width = blocks * LO * TILE
    return [pltpu.VMEM((LO * padded, width), BF16), pltpu.VMEM((width, rows_here // LO), BF16)]


def place_first(received, rows_here, classes, padded):
    blocks = len(received)

    def kernel(*refs):
        out_ref, x_ref, hot_ref = refs[blocks:]
        out_ref[...] = placed(refs[:blocks], x_ref, hot_ref, rows_here, classes, padded)

    flops = 2 * LO * padded * rows_here * blocks * TILE
    return call(
        kernel,
        [shape((LO * padded, rows_here // LO), F32)],
        [VMEM] * blocks,
        place_scratch(blocks, rows_here, padded),
        flops=flops,
        nbytes=4 * LO * padded * rows_here // LO,
        name="place_first",
    )(*received)[0]


def place_scores(first, received, rows_here, classes, padded):
    blocks = len(received)
    tiles = rows_here // TILE

    def kernel(*refs):
        first_ref = refs[0]
        raised_ref, total_ref, x_ref, hot_ref = refs[1 + blocks :]
        logits = placed(refs[1 : 1 + blocks], x_ref, hot_ref, rows_here, classes, padded)
        logits = logits + first_ref[...]
        row = iota((padded, TILE), 0)
        for i in range(tiles):
            q, c = divmod(i, tiles // LO)
            part = logits[q * padded : (q + 1) * padded, c * TILE : (c + 1) * TILE]
            raised = jnp.where(row < classes, jnp.exp(part), 0.0)
            raised_ref[i] = raised
            total_ref[i : i + 1, :] = jnp.sum(raised, axis=0, keepdims=True)

    return call(
        kernel,
        [shape((tiles, padded, TILE), F32), shape((tiles, TILE), F32)],
        [VMEM] * (1 + blocks),
        place_scratch(blocks, rows_here, padded),
        name="place_scores",
    )(first, *received)


def exported_columns(moved_tiles, export_row, padded):
    source = jnp.concatenate(moved_tiles, axis=1)
    rows = source.shape[1]
    hot = jnp.where(iota((rows, TILE), 0) == export_row, 1.0, 0.0).astype(BF16)
    return jnp.dot(source, hot, preferred_element_type=F32).astype(BF16)


def start_residuals(raised, totals, labels, mask, exports, ids):
    tiles, padded, _ = raised.shape
    count = len(totals)

    def kernel(ids_ref, raised_ref, *refs):
        total_refs = refs[:count]
        label_ref, mask_ref, export_ref, base_ref, start_ref, moved_ref, out_ref = refs[count:]
        total = total_refs[0][...]
        for other in total_refs[1:]:
            total = total + other[...]
        ids = ids_ref[...]
        moved = []
        for i in range(tiles):
            base = raised_ref[i] / total[i : i + 1, :]
            truth = jnp.where(ids == label_ref[i : i + 1, :], 1.0, 0.0)
            start = mask_ref[i : i + 1, :].astype(F32) * (truth - base)
            base_ref[i] = base
            start_ref[i] = start
            moved.append(start.astype(BF16))
            moved_ref[i] = moved[-1]
        out_ref[...] = exported_columns(moved, export_ref[...], padded)

    full = shape((tiles, padded, TILE), F32)
    outs = [full, full, shape((tiles, padded, TILE), BF16), shape((padded, TILE), BF16)]
    return call(kernel, outs, [VMEM] * (count + 5), name="start_residuals")(
        ids, raised, *totals, labels, mask, exports
    )


def pair_products(table_ref, kind, s_ref, a_ref, acc_ref):
    acc_ref[...] = jnp.zeros_like(acc_ref)

    def product(k):
        slots = [table_ref[kind, 0, k], table_ref[kind, 0, k + 1]]
        sources = [table_ref[kind, 1, k], table_ref[kind, 1, k + 1]]
        left = jnp.concatenate([s_ref[j] for j in sources], axis=1)
        right = jnp.concatenate([a_ref[t] for t in slots], axis=1)
        acc_ref[table_ref[kind, 2, k]] += lax.dot_general(
            left, right, (((1,), (1,)), ((), ())), preferred_element_type=F32
        )

    def several(first, count):
        def step(group, carry):
            for u in range(count):
                product(2 * (first + group * count + u))
            return carry

        return step

    groups = table_ref[kind, 3, 0]
    lax.fori_loop(0, groups, several(0, GROUP), 0)
    lax.fori_loop(0, table_ref[kind, 3, 1], several(groups * GROUP, REST), 0)


def own_products(table, moved, adjacency):
    tiles, padded, _ = moved.shape

    def kernel(t_ref, moved_ref, a_ref, acc_ref, s_ref):
        s_ref[0] = jnp.zeros((padded, TILE), BF16)
        for i in range(tiles):
            s_ref[1 + i] = moved_ref[i]
        pair_products(t_ref, 0, s_ref, a_ref, acc_ref)

    return call(
        kernel,
        shape((tiles, padded, TILE), F32),
        [SMEM, VMEM, VMEM],
        [pltpu.VMEM((1 + tiles, padded, TILE), BF16)],
        name="own_products",
    )(in_smem(table), moved, adjacency)


def hop(table, boundary, adjacency, own, start, exports, last):
    tiles, padded, _ = start.shape
    count = len(boundary)
    sources = sum(b.shape[0] for b in boundary)

    def kernel(*refs):
        t_ref = refs[0]
        boundary_refs = refs[1 : 1 + count]
        a_ref, own_ref, start_ref, export_ref, first_out, second_out, s_ref, acc_ref = refs[1 + count :]
        s_ref[0] = jnp.zeros((padded, TILE), BF16)
        at = 1
        for ref in boundary_refs:
            for k in range(ref.shape[0]):
                s_ref[at] = ref[k]
                at += 1
        pair_products(t_ref, 1, s_ref, a_ref, acc_ref)
        moved_out = []
        for i in range(tiles):
            spread = own_ref[i] + acc_ref[i]
            residual = (1.0 - alpha_mix) * start_ref[i] + alpha_mix * spread
            if last:
                first_out[i] = residual
                second_out[i : i + 1, :] = jnp.sum(residual * residual, axis=0, keepdims=True)
            else:
                moved_out.append(residual.astype(BF16))
                first_out[i] = moved_out[-1]
        if not last:
            second_out[...] = exported_columns(moved_out, export_ref[...], padded)

    if last:
        outs = [shape((tiles, padded, TILE), F32), shape((tiles, TILE), F32)]
    else:
        outs = [shape((tiles, padded, TILE), BF16), shape((padded, TILE), BF16)]
    return call(
        kernel,
        outs,
        [SMEM] + [VMEM] * (count + 4),
        [pltpu.VMEM((1 + sources, padded, TILE), BF16), pltpu.VMEM((tiles, padded, TILE), F32)],
        name="hop",
    )(in_smem(table), *boundary, adjacency, own, start, exports)


def blend_terms(base, residual, labels, mask, gain, ids):
    tiles, padded, _ = base.shape

    def kernel(ids_ref, base_ref, residual_ref, label_ref, mask_ref, gain_ref, term_ref, factor_ref):
        ids = ids_ref[...]
        gains = gain_ref[...]
        for i in range(tiles):
            truth = jnp.where(ids == label_ref[i : i + 1, :], 1.0, 0.0)
            trained = mask_ref[i : i + 1, :] == 1
            term_ref[i] = jnp.where(trained, truth, base_ref[i])
            factor_ref[i] = jnp.where(trained, 0.0, gains * residual_ref[i])

    full = shape((tiles, padded, TILE), F32)
    return call(kernel, [full, full], [VMEM] * 6, name="blend_terms")(
        ids, base, residual, labels, mask, gain
    )


def blend(term, factor, squares, classes, class_total):
    tiles, padded, _ = term.shape
    count = len(squares)
    cuts = 4
    each = tiles // cuts

    def kernel(term_ref, factor_ref, *refs):
        square_refs = refs[:count]
        out_hbm, out_ref, sems = refs[count:]
        total = square_refs[0][...]
        for other in square_refs[1:]:
            total = total + other[...]
        inverse = lax.rsqrt(total / float(class_total) + spread_eps)
        copies = []
        for cut in range(cuts):
            for i in range(cut * each, (cut + 1) * each):
                blended = term_ref[i] + factor_ref[i] * inverse[i : i + 1, :]
                out_ref[:, i * TILE : (i + 1) * TILE] = blended[:classes]
            cols = pl.ds(cut * each * TILE, each * TILE)
            copy = pltpu.make_async_copy(out_ref.at[:, cols], out_hbm.at[:, cols], sems.at[cut])
            copy.start()
            copies.append(copy)
        for copy in copies:
            copy.wait()

    return call(
        kernel,
        shape((classes, tiles * TILE), F32),
        [VMEM] * (count + 2),
        [pltpu.VMEM((classes, tiles * TILE), F32), pltpu.SemaphoreType.DMA((cuts,))],
        name="blend",
        where=HBM,
    )(term, factor, *squares)


def exchanged(value, axis, count, step):
    return lax.ppermute(value, axis, [(i, step_between(i, step, count)) for i in range(count)])


def from_all(value, axis):
    count = lax.axis_size(axis)
    return [value] + [exchanged(value, axis, count, step) for step in range(1, count)]


def shards(
    features,
    class_weight,
    class_bias,
    part_position,
    labels,
    train_mask,
    export_rows,
    tile_coords,
    tile_count,
    adjacency,
    corr_gain,
):
    node_count = lax.axis_size("node")
    row_count = lax.axis_size("row")
    part_count = node_count * row_count
    rows_here = part_position.shape[0]
    classes = class_bias.shape[0]
    class_total = classes * lax.axis_size("cls")
    padded = up(classes + 1, 16)
    tiles = rows_here // TILE
    capacity = 2 * rows_here // part_count
    counts = (node_count, row_count)
    labels = labels.reshape(tiles, TILE)
    mask = train_mask.reshape(tiles, TILE)
    weight = class_weight.T
    share = capacity // LO
    direct = share == TILE
    parts = partial_scores(features, weight, row_count, rows_here, padded)
    partials = [
        exchanged(parts[step - 1], "row", row_count, step) for step in range(1, row_count)
    ]
    rest = (labels, mask, export_rows, class_bias[None], corr_gain[None], adjacency[0])
    score, aux, hot, table, labels, mask, exports, bias, gain, adjacency, ids = own_tables(
        features,
        weight,
        part_position.reshape(tiles, TILE),
        tile_coords[0],
        tile_count,
        rest,
        counts,
        padded,
        capacity,
        direct,
    )
    sending = compact_scores([score] + partials, bias, aux, hot, classes, padded)
    if direct:
        axes = ("node", "row")
        received = [sending[0]] + [
            exchanged(sending[step], axes, part_count, step) for step in [1, *range(part_count - 1, 1, -1)]
        ]
    else:
        blocks, width = len(sending), sending[0].shape[0]
        sent = jnp.stack(sending)
        sent = sent.reshape(blocks, width, TILE // share, share).transpose(0, 2, 1, 3)
        sent = sent.reshape(part_count, width, share)
        got = lax.all_to_all(sent, ("node", "row"), split_axis=0, concat_axis=0, tiled=True)
        got = got.reshape(blocks, TILE // share, width, share).transpose(0, 2, 1, 3)
        got = got.reshape(blocks, width, TILE)
        received = [got[s] for s in range(blocks)]
    first = place_first(received[:FIRST], rows_here, classes, padded)
    raised, total = place_scores(first, received[FIRST:], rows_here, classes, padded)
    totals = from_all(total, "cls")
    base, start, moved, out = start_residuals(
        raised, totals, labels, mask, exports, ids
    )
    for index in range(HOPS):
        group = jnp.stack(from_all(out, "row"))
        own = own_products(table, moved, adjacency)
        group, own = lax.optimization_barrier((group, own))
        boundary = from_all(group, "node")
        moved, out = hop(
            table, boundary, adjacency, own, start, exports, index == HOPS - 1
        )
    squares = from_all(out, "cls")
    term, factor = blend_terms(base, moved, labels, mask, gain, ids)
    return blend(term, factor, squares, classes, class_total)


def solution(mesh):
    in_specs = (
        P("row", "node"),
        P("row", "cls"),
        P("cls"),
        P(("node", "row")),
        P(("node", "row")),
        P(("node", "row")),
        P(("node", "row"), None),
        P(("node", "row"), None, None),
        P(("node", "row")),
        P(("node", "row"), None, None, None),
        P("cls"),
    )
    out_specs = P("cls", ("node", "row"))
    return jax.shard_map(shards, mesh=mesh, in_specs=in_specs, out_specs=out_specs, check_vma=False)
```

```python
import jax
import jax.numpy as jnp
from jax import lax
from jax.experimental import pallas as pl
from jax.experimental.pallas import tpu as pltpu
from jax.sharding import PartitionSpec as P

HOPS = 2
TILE = 128
LO = 4
GROUP = 16
REST = 4
FIRST = 5

alpha_mix = 0.8
spread_eps = 1e-06

F32 = jnp.float32
BF16 = jnp.bfloat16
I32 = jnp.int32
VMEM = pl.BlockSpec(memory_space=pltpu.VMEM)
HBM = pl.BlockSpec(memory_space=pltpu.HBM)
SMEM = pl.BlockSpec(memory_space=pltpu.SMEM)


def iota(shape, dim):
    return lax.broadcasted_iota(I32, shape, dim)


def call(kernel, outs, ins, scratch=(), mb=12, flops=0, nbytes=0, name=None, where=None):
    return pl.pallas_call(
        kernel,
        out_shape=outs,
        in_specs=ins,
        out_specs=where or jax.tree.map(lambda _: VMEM, outs),
        scratch_shapes=list(scratch),
        compiler_params=pltpu.CompilerParams(vmem_limit_bytes=mb << 20),
        cost_estimate=pl.CostEstimate(flops=flops, bytes_accessed=nbytes, transcendentals=0),
        name=name,
    )


def in_hbm(*arrays):
    return [pltpu.with_memory_space_constraint(x, pltpu.HBM) for x in arrays]


def in_smem(x):
    return pltpu.with_memory_space_constraint(x, pltpu.SMEM)


def shape(dims, dtype):
    return jax.ShapeDtypeStruct(dims, dtype)


def up(value, step):
    return -(-value // step) * step


def step_between(a, b, count):
    assert count & (count - 1) == 0
    return a ^ b


def padded_weight(weight, padded):
    classes, depth = weight.shape
    weight = weight.astype(F32)
    return jnp.concatenate([weight, jnp.zeros((padded - classes, depth), F32)], axis=0).astype(BF16)


def node_block(ref, step, row_count, rows_here):
    at = step_between(lax.axis_index("row").astype(I32), step, row_count) * rows_here
    return ref.at[:, pl.ds(pl.multiple_of(at, TILE), rows_here)]


def partial_scores(features, weight, row_count, rows_here, padded):
    classes, depth = weight.shape
    steps = range(1, row_count)

    def kernel(f_hbm, w_hbm, *refs):
        outs = refs[: row_count - 1]
        f_ref, w_ref, sems = refs[row_count - 1 :]
        copies = [pltpu.make_async_copy(w_hbm, w_ref, sems.at[0])]
        for step in steps:
            source = node_block(f_hbm, step, row_count, rows_here)
            copies.append(pltpu.make_async_copy(source, f_ref.at[step - 1], sems.at[step]))
        for copy in copies:
            copy.start()
        copies[0].wait()
        w = padded_weight(w_ref[...], padded)
        for step in steps:
            copies[step].wait()
            score = jnp.dot(w, f_ref[step - 1], preferred_element_type=F32)
            outs[step - 1][...] = score.astype(BF16)

    out = shape((padded, rows_here), BF16)
    scratch = [
        pltpu.VMEM((row_count - 1, depth, rows_here), BF16),
        pltpu.VMEM((classes, depth), BF16),
        pltpu.SemaphoreType.DMA((row_count,)),
    ]
    return call(
        kernel, [out] * (row_count - 1), [HBM, HBM], scratch, name="partial_scores"
    )(*in_hbm(features, weight))


def slot_tables(pos, me, rows_here, part_count, capacity, aux_ref, hot_ref):
    tiles = rows_here // TILE
    share = capacity // LO
    columns = part_count * share
    block = pos // rows_here
    before = (iota((TILE, TILE), 0) < iota((TILE, TILE), 1)).astype(BF16)
    ones = jnp.ones((TILE, TILE), BF16)
    above = (iota((tiles, tiles), 1) < iota((tiles, tiles), 0)).astype(BF16)
    rank = jnp.zeros((tiles, TILE), F32)
    for d in range(part_count):
        member = block == d
        m = member.astype(F32).astype(BF16)
        inside = jnp.dot(m, before, preferred_element_type=F32)
        each = jnp.dot(m, ones, preferred_element_type=F32).astype(BF16)
        offset = jnp.dot(above, each, preferred_element_type=F32)
        rank = jnp.where(member, inside + offset, rank)
    rank = rank.astype(I32)
    low = rank // share
    column = step_between(block, me, part_count) * share + (rank - low * share)
    place = pos - block * rows_here
    power = place // TILE
    scale = jnp.ones((tiles, TILE), F32)
    for j in range(1, tiles):
        scale = jnp.where(power >= j, 2.0 * scale, scale)
    aux_ref[0] = low.astype(F32)
    aux_ref[1] = (place - power * TILE + TILE).astype(F32) * scale
    turned = jnp.concatenate([column, jnp.zeros((TILE - tiles, TILE), I32)], axis=0)
    turned = turned.astype(F32).T.astype(I32)
    across = iota((TILE, columns), 1)
    for j in range(tiles):
        hot = jnp.where(across == turned[:, j : j + 1], 1.0, 0.0)
        hot_ref[j * TILE : (j + 1) * TILE, :] = hot.astype(BF16)


def pair_tables(coords, live, here, counts, row_tiles, table_ref):
    node_count, row_count = counts
    slots = coords.shape[1]
    places = up(slots + row_tiles, 2 * REST)
    row = coords[0:1, :]
    column = coords[1:2, :]
    slot = iota((1, slots), 1)
    part = jnp.maximum(column - row_tiles, 0)
    part_node = part // row_count
    part_row = part - part_node * row_count
    node_step = step_between(part_node, here[0], node_count)
    row_step = step_between(part_row, here[1], row_count)
    before = (iota((slots, slots), 0) < iota((slots, slots), 1)).astype(BF16)
    ones = jnp.ones((slots, slots), BF16)
    above = (iota((row_tiles, row_tiles), 1) < iota((row_tiles, row_tiles), 0)).astype(BF16)
    line = iota((8, slots), 0)
    lane = iota((8, places), 1)
    for kind in range(2):
        if kind == 0:
            source = column
            wanted = column < row_tiles
        else:
            source = node_step * row_count + row_step
            wanted = column >= row_tiles
        member = (iota((row_tiles, slots), 0) == row) & (slot < live) & wanted
        m = jnp.where(member, 1.0, 0.0).astype(BF16)
        rank = jnp.dot(m, before, preferred_element_type=F32)
        number = jnp.dot(m, ones, preferred_element_type=F32).astype(I32)
        pairs = ((number + 1) // 2).astype(F32)
        first = jnp.dot(above, pairs.astype(BF16), preferred_element_type=F32)
        place = jnp.sum(jnp.where(member, 2.0 * first + rank + 1.0, 0.0), axis=0, keepdims=True)
        place = place.astype(I32) - 1
        hot = jnp.where(iota((places, slots), 0) == place, 1.0, 0.0).astype(BF16)
        values = jnp.where(
            line == 0, slot, jnp.where(line == 1, source + 1, jnp.where(line == 2, row, 0))
        )
        table = lax.dot_general(
            values.astype(F32).astype(BF16), hot, (((1,), (1,)), ((), ())), preferred_element_type=F32
        )
        total = jnp.sum(pairs, axis=0, keepdims=True).astype(I32)[:, :1]
        groups = total // GROUP
        rest = (total - groups * GROUP + REST - 1) // REST
        sizes = jnp.where(lane == 0, groups, rest)
        table_ref[kind] = jnp.where(iota((8, places), 0) == 3, sizes, table.astype(I32))


def own_tables(features, weight, positions, coords, live, rest, counts, padded, capacity, direct):
    node_count, row_count = counts
    classes, depth = weight.shape
    tiles = positions.shape[0]
    rows_here = tiles * TILE
    part_count = node_count * row_count
    columns = part_count * capacity // LO
    labels, mask, exports, bias, gain, adjacency = rest
    slots = adjacency.shape[0]

    def kernel(live_ref, *refs):
        node, row = lax.axis_index("node").astype(I32), lax.axis_index("row").astype(I32)
        f_hbm, w_hbm, p_hbm, c_hbm, l_hbm, m_hbm, e_hbm, b_hbm, g_hbm, a_hbm = refs[:10]
        score_ref, aux_ref, hot_ref, table_out, l_ref, m_ref, e_out, b_out, g_out, a_ref, i_out = refs[10:21]
        f_ref, w_ref, p_ref, c_ref, b_ref, g_ref, t_ref, e_ref, sems = refs[21:]
        source = node_block(f_hbm, 0, row_count, rows_here)
        pairs = [
            (p_hbm, p_ref),
            (c_hbm, c_ref),
            (b_hbm, b_ref),
            (g_hbm, g_ref),
            (e_hbm, e_ref),
            (w_hbm, w_ref),
            (source, f_ref),
            (l_hbm, l_ref),
            (m_hbm, m_ref),
            (a_hbm, a_ref),
        ]
        copies = [pltpu.make_async_copy(a, b, sems.at[i]) for i, (a, b) in enumerate(pairs)]
        for copy in copies:
            copy.start()
        for copy in copies[:5]:
            copy.wait()
        me = node * row_count + row if direct else 0
        slot_tables(p_ref[...], me, rows_here, part_count, capacity, aux_ref, hot_ref)
        pair_tables(c_ref[...], live_ref[0], (node, row), counts, tiles, t_ref)
        table_copy = pltpu.make_async_copy(t_ref, table_out, sems.at[10])
        table_copy.start()
        b_out[...] = jnp.broadcast_to(turned_column(b_ref[...], padded), (padded, TILE))
        g_out[...] = jnp.broadcast_to(turned_column(g_ref[...], padded), (padded, TILE))
        chosen = iota((rows_here, TILE), 0) == e_ref[...]
        e_out[...] = jnp.where(chosen, 1.0, 0.0).astype(BF16)
        line = iota((padded, TILE), 0)
        first = lax.axis_index("cls").astype(I32) * classes
        i_out[...] = jnp.where(line < classes, line + first, -1)
        table_copy.wait()
        for copy in copies[5:]:
            copy.wait()
        w = padded_weight(w_ref[...], padded)
        score_ref[...] = jnp.dot(w, f_ref[...], preferred_element_type=F32).astype(BF16)

    like = [shape(x.shape, x.dtype) for x in rest]
    outs = [
        shape((padded, rows_here), BF16),
        shape((2, tiles, TILE), F32),
        shape((rows_here, columns), BF16),
        pltpu.SMEM((2, 8, up(slots + tiles, 2 * REST)), I32),
        like[0],
        like[1],
        shape((rows_here, TILE), BF16),
        shape((padded, TILE), F32),
        shape((padded, TILE), F32),
        like[5],
        shape((padded, TILE), I32),
    ]
    scratch = [
        pltpu.VMEM((depth, rows_here), BF16),
        pltpu.VMEM((classes, depth), BF16),
        pltpu.VMEM(positions.shape, I32),
        pltpu.VMEM(coords.shape, I32),
        pltpu.VMEM(bias.shape, F32),
        pltpu.VMEM(gain.shape, F32),
        pltpu.VMEM(outs[3].shape, I32),
        pltpu.VMEM(exports.shape, I32),
        pltpu.SemaphoreType.DMA((11,)),
    ]
    where = [VMEM] * 3 + [SMEM] + [VMEM] * 7
    return call(kernel, outs, [SMEM] + [HBM] * 10, scratch, name="own_tables", where=where)(
        live, *in_hbm(features, weight, positions, coords, *rest)
    )


def turned_column(row, padded):
    row = jnp.concatenate([row, jnp.zeros((1, TILE - row.shape[1]), F32)], axis=1)
    return jnp.broadcast_to(row, (8, TILE)).T[:padded, 0:1]


def laid_block(laid, at, rows, padded):
    block = laid[:, at * TILE : (at + 1) * TILE]
    kept = jnp.concatenate([block[l * padded : l * padded + rows] for l in range(LO)], axis=0)
    return kept.astype(BF16)


def compact_scores(partials, bias, aux, hot, classes, padded):
    count = len(partials)
    rows_here = partials[0].shape[1]
    tiles = rows_here // TILE
    rows = classes + 1

    def kernel(*refs):
        parts = refs[:count]
        b_ref, aux_ref, hot_ref = refs[count : count + 3]
        outs, x_ref = refs[count + 3 : -1], refs[-1]
        bias_column = b_ref[...]
        row = iota((padded, TILE), 0)
        for j in range(tiles):
            cols = slice(j * TILE, (j + 1) * TILE)
            total = parts[0][:, cols].astype(F32)
            for other in parts[1:]:
                total = total + other[:, cols].astype(F32)
            value = (total + bias_column).astype(BF16).astype(F32)
            low = aux_ref[0, j : j + 1, :]
            value = jnp.where(row == classes, aux_ref[1, j : j + 1, :], value)
            for l in range(LO):
                x_ref[l * padded : (l + 1) * padded, cols] = jnp.where(low == l, value, 0.0).astype(BF16)
        laid = jnp.dot(x_ref[...], hot_ref[...], preferred_element_type=F32)
        for d, out in enumerate(outs):
            out[...] = laid_block(laid, d, rows, padded)

    return call(
        kernel,
        [shape((LO * rows, TILE), BF16)] * (hot.shape[1] // TILE),
        [VMEM] * (count + 3),
        [pltpu.VMEM((LO * padded, rows_here), BF16)],
        name="compact_scores",
    )(*partials, bias, aux, hot)


def placed(r_refs, x_ref, hot_ref, rows_here, classes, padded):
    rows = classes + 1
    high = rows_here // LO
    blocks = len(r_refs)
    width = LO * rows
    pick = iota((8, width), 1) - iota((8, width), 0) * rows == classes
    pick = jnp.where(pick & (iota((8, width), 0) < LO), 1.0, 0.0).astype(BF16)
    held = [jnp.dot(pick, ref[...], preferred_element_type=F32) for ref in r_refs]
    held = jnp.concatenate(held, axis=0)
    power = jnp.zeros(held.shape, I32)
    scale = jnp.ones(held.shape, F32)
    for j in range(1, rows_here // TILE):
        above = held >= float(TILE << j)
        power = jnp.where(above, j, power)
        scale = jnp.where(above, 0.5**j, scale)
    code = jnp.where(held > 0.0, power * TILE + (held * scale).astype(I32) - TILE, -1)
    group = jnp.where(code < 0, -1, code // high)
    inner = (code & (high - 1)).astype(F32)
    rest = jnp.zeros((TILE - 8 * blocks, TILE), F32)
    turned = jnp.concatenate([inner, rest], axis=0).T.astype(I32)
    across = iota((TILE, high), 1)
    tail = jnp.zeros((padded - rows, TILE), F32)
    for s in range(blocks):
        block = r_refs[s][...].astype(F32)
        for l in range(LO):
            at = (s * LO + l) * TILE
            lane = s * 8 + l
            hot = jnp.where(across == turned[:, lane : lane + 1], 1.0, 0.0)
            hot_ref[at : at + TILE, :] = hot.astype(BF16)
            value = jnp.concatenate([block[l * rows : (l + 1) * rows], tail], axis=0)
            mine = group[lane : lane + 1, :]
            for q in range(LO):
                x_ref[q * padded : (q + 1) * padded, at : at + TILE] = jnp.where(
                    mine == q, value, 0.0
                ).astype(BF16)
    return jnp.dot(x_ref[...], hot_ref[...], preferred_element_type=F32)


def place_scratch(blocks, rows_here, padded):
    width = blocks * LO * TILE
    return [pltpu.VMEM((LO * padded, width), BF16), pltpu.VMEM((width, rows_here // LO), BF16)]


def place_first(received, rows_here, classes, padded):
    blocks = len(received)

    def kernel(*refs):
        out_ref, x_ref, hot_ref = refs[blocks:]
        out_ref[...] = placed(refs[:blocks], x_ref, hot_ref, rows_here, classes, padded)

    flops = 2 * LO * padded * rows_here * blocks * TILE
    return call(
        kernel,
        [shape((LO * padded, rows_here // LO), F32)],
        [VMEM] * blocks,
        place_scratch(blocks, rows_here, padded),
        flops=flops,
        nbytes=4 * LO * padded * rows_here // LO,
        name="place_first",
    )(*received)[0]


def place_scores(first, received, rows_here, classes, padded):
    blocks = len(received)
    tiles = rows_here // TILE

    def kernel(*refs):
        first_ref = refs[0]
        raised_ref, total_ref, x_ref, hot_ref = refs[1 + blocks :]
        logits = placed(refs[1 : 1 + blocks], x_ref, hot_ref, rows_here, classes, padded)
        logits = logits + first_ref[...]
        row = iota((padded, TILE), 0)
        for i in range(tiles):
            q, c = divmod(i, tiles // LO)
            part = logits[q * padded : (q + 1) * padded, c * TILE : (c + 1) * TILE]
            raised = jnp.where(row < classes, jnp.exp(part), 0.0)
            raised_ref[i] = raised
            total_ref[i : i + 1, :] = jnp.sum(raised, axis=0, keepdims=True)

    return call(
        kernel,
        [shape((tiles, padded, TILE), F32), shape((tiles, TILE), F32)],
        [VMEM] * (1 + blocks),
        place_scratch(blocks, rows_here, padded),
        name="place_scores",
    )(first, *received)


def exported_columns(moved_tiles, chosen):
    source = jnp.concatenate(moved_tiles, axis=1)
    return jnp.dot(source, chosen, preferred_element_type=F32).astype(BF16)


def start_residuals(raised, totals, labels, mask, exports, ids):
    tiles, padded, _ = raised.shape
    count = len(totals)

    def kernel(ids_ref, raised_ref, *refs):
        total_refs = refs[:count]
        label_ref, mask_ref, export_ref, base_ref, start_ref, moved_ref, out_ref = refs[count:]
        total = total_refs[0][...]
        for other in total_refs[1:]:
            total = total + other[...]
        ids = ids_ref[...]
        moved = []
        for i in range(tiles):
            base = raised_ref[i] / total[i : i + 1, :]
            truth = jnp.where(ids == label_ref[i : i + 1, :], 1.0, 0.0)
            start = mask_ref[i : i + 1, :].astype(F32) * (truth - base)
            base_ref[i] = base
            start_ref[i] = start
            moved.append(start.astype(BF16))
            moved_ref[i] = moved[-1]
        out_ref[...] = exported_columns(moved, export_ref[...])

    full = shape((tiles, padded, TILE), F32)
    outs = [full, full, shape((tiles, padded, TILE), BF16), shape((padded, TILE), BF16)]
    return call(kernel, outs, [VMEM] * (count + 5), name="start_residuals")(
        ids, raised, *totals, labels, mask, exports
    )


def pair_products(table_ref, kind, s_ref, a_ref, acc_ref):
    acc_ref[...] = jnp.zeros_like(acc_ref)

    def product(k):
        slots = [table_ref[kind, 0, k], table_ref[kind, 0, k + 1]]
        sources = [table_ref[kind, 1, k], table_ref[kind, 1, k + 1]]
        left = jnp.concatenate([s_ref[j] for j in sources], axis=1)
        right = jnp.concatenate([a_ref[t] for t in slots], axis=1)
        acc_ref[table_ref[kind, 2, k]] += lax.dot_general(
            left, right, (((1,), (1,)), ((), ())), preferred_element_type=F32
        )

    def several(first, count):
        def step(group, carry):
            for u in range(count):
                product(2 * (first + group * count + u))
            return carry

        return step

    groups = table_ref[kind, 3, 0]
    lax.fori_loop(0, groups, several(0, GROUP), 0)
    lax.fori_loop(0, table_ref[kind, 3, 1], several(groups * GROUP, REST), 0)


def own_products(table, moved, adjacency):
    tiles, padded, _ = moved.shape

    def kernel(t_ref, moved_ref, a_ref, acc_ref, s_ref):
        s_ref[0] = jnp.zeros((padded, TILE), BF16)
        for i in range(tiles):
            s_ref[1 + i] = moved_ref[i]
        pair_products(t_ref, 0, s_ref, a_ref, acc_ref)

    return call(
        kernel,
        shape((tiles, padded, TILE), F32),
        [SMEM, VMEM, VMEM],
        [pltpu.VMEM((1 + tiles, padded, TILE), BF16)],
        name="own_products",
    )(in_smem(table), moved, adjacency)


def hop(table, boundary, adjacency, own, start, exports, last):
    tiles, padded, _ = start.shape
    count = len(boundary)
    sources = sum(b.shape[0] for b in boundary)

    def kernel(*refs):
        t_ref = refs[0]
        boundary_refs = refs[1 : 1 + count]
        a_ref, own_ref, start_ref, export_ref, first_out, second_out, s_ref, acc_ref = refs[1 + count :]
        s_ref[0] = jnp.zeros((padded, TILE), BF16)
        at = 1
        for ref in boundary_refs:
            for k in range(ref.shape[0]):
                s_ref[at] = ref[k]
                at += 1
        pair_products(t_ref, 1, s_ref, a_ref, acc_ref)
        moved_out = []
        for i in range(tiles):
            spread = own_ref[i] + acc_ref[i]
            residual = (1.0 - alpha_mix) * start_ref[i] + alpha_mix * spread
            if last:
                first_out[i] = residual
                second_out[i : i + 1, :] = jnp.sum(residual * residual, axis=0, keepdims=True)
            else:
                moved_out.append(residual.astype(BF16))
                first_out[i] = moved_out[-1]
        if not last:
            second_out[...] = exported_columns(moved_out, export_ref[...])

    if last:
        outs = [shape((tiles, padded, TILE), F32), shape((tiles, TILE), F32)]
    else:
        outs = [shape((tiles, padded, TILE), BF16), shape((padded, TILE), BF16)]
    return call(
        kernel,
        outs,
        [SMEM] + [VMEM] * (count + 4),
        [pltpu.VMEM((1 + sources, padded, TILE), BF16), pltpu.VMEM((tiles, padded, TILE), F32)],
        name="hop",
    )(in_smem(table), *boundary, adjacency, own, start, exports)


def blend_terms(base, residual, labels, mask, gain, ids):
    tiles, padded, _ = base.shape

    def kernel(ids_ref, base_ref, residual_ref, label_ref, mask_ref, gain_ref, term_ref, factor_ref):
        ids = ids_ref[...]
        gains = gain_ref[...]
        for i in range(tiles):
            truth = jnp.where(ids == label_ref[i : i + 1, :], 1.0, 0.0)
            trained = mask_ref[i : i + 1, :] == 1
            term_ref[i] = jnp.where(trained, truth, base_ref[i])
            factor_ref[i] = jnp.where(trained, 0.0, gains * residual_ref[i])

    full = shape((tiles, padded, TILE), F32)
    return call(kernel, [full, full], [VMEM] * 6, name="blend_terms")(
        ids, base, residual, labels, mask, gain
    )


def blend(term, factor, squares, classes, class_total):
    tiles, padded, _ = term.shape
    count = len(squares)
    cuts = 4
    each = tiles // cuts

    def kernel(term_ref, factor_ref, *refs):
        square_refs = refs[:count]
        out_hbm, out_ref, sems = refs[count:]
        total = square_refs[0][...]
        for other in square_refs[1:]:
            total = total + other[...]
        inverse = lax.rsqrt(total / float(class_total) + spread_eps)
        copies = []
        for cut in range(cuts):
            for i in range(cut * each, (cut + 1) * each):
                blended = term_ref[i] + factor_ref[i] * inverse[i : i + 1, :]
                out_ref[:, i * TILE : (i + 1) * TILE] = blended[:classes]
            cols = pl.ds(cut * each * TILE, each * TILE)
            copy = pltpu.make_async_copy(out_ref.at[:, cols], out_hbm.at[:, cols], sems.at[cut])
            copy.start()
            copies.append(copy)
        for copy in copies:
            copy.wait()

    return call(
        kernel,
        shape((classes, tiles * TILE), F32),
        [VMEM] * (count + 2),
        [pltpu.VMEM((classes, tiles * TILE), F32), pltpu.SemaphoreType.DMA((cuts,))],
        name="blend",
        where=HBM,
    )(term, factor, *squares)


def exchanged(value, axis, count, step):
    return lax.ppermute(value, axis, [(i, step_between(i, step, count)) for i in range(count)])


def from_all(value, axis):
    count = lax.axis_size(axis)
    steps = sorted(range(1, count), key=lambda step: (step + 1) % 4 if axis == "node" else step)
    got = {step: exchanged(value, axis, count, step) for step in steps}
    return [value] + [got[step] for step in range(1, count)]


def shards(
    features,
    class_weight,
    class_bias,
    part_position,
    labels,
    train_mask,
    export_rows,
    tile_coords,
    tile_count,
    adjacency,
    corr_gain,
):
    node_count = lax.axis_size("node")
    row_count = lax.axis_size("row")
    part_count = node_count * row_count
    rows_here = part_position.shape[0]
    classes = class_bias.shape[0]
    class_total = classes * lax.axis_size("cls")
    padded = up(classes + 1, 16)
    tiles = rows_here // TILE
    capacity = 2 * rows_here // part_count
    counts = (node_count, row_count)
    labels = labels.reshape(tiles, TILE)
    mask = train_mask.reshape(tiles, TILE)
    weight = class_weight.T
    share = capacity // LO
    direct = share == TILE
    parts = partial_scores(features, weight, row_count, rows_here, padded)
    partials = [
        exchanged(parts[step - 1], "row", row_count, step) for step in range(1, row_count)
    ]
    rest = (labels, mask, export_rows, class_bias[None], corr_gain[None], adjacency[0])
    score, aux, hot, table, labels, mask, exports, bias, gain, adjacency, ids = own_tables(
        features,
        weight,
        part_position.reshape(tiles, TILE),
        tile_coords[0],
        tile_count,
        rest,
        counts,
        padded,
        capacity,
        direct,
    )
    sending = compact_scores([score] + partials, bias, aux, hot, classes, padded)
    if direct:
        axes = ("node", "row")
        received = [sending[0]] + [
            exchanged(sending[step], axes, part_count, step) for step in ([2, 7, 6, 5, 4, 3, 1] if part_count == 8 else range(1, part_count))
        ]
    else:
        blocks, width = len(sending), sending[0].shape[0]
        sent = jnp.stack(sending)
        sent = sent.reshape(blocks, width, TILE // share, share).transpose(0, 2, 1, 3)
        sent = sent.reshape(part_count, width, share)
        got = lax.all_to_all(sent, ("node", "row"), split_axis=0, concat_axis=0, tiled=True)
        got = got.reshape(blocks, TILE // share, width, share).transpose(0, 2, 1, 3)
        got = got.reshape(blocks, width, TILE)
        received = [got[s] for s in range(blocks)]
    first = place_first(received[:FIRST], rows_here, classes, padded)
    raised, total = place_scores(first, received[FIRST:], rows_here, classes, padded)
    totals = from_all(total, "cls")
    base, start, moved, out = start_residuals(
        raised, totals, labels, mask, exports, ids
    )
    for index in range(HOPS):
        group = jnp.stack(from_all(out, "row"))
        own = own_products(table, moved, adjacency)
        group, own = lax.optimization_barrier((group, own))
        boundary = from_all(group, "node")
        moved, out = hop(
            table, boundary, adjacency, own, start, exports, index == HOPS - 1
        )
    squares = from_all(out, "cls")
    term, factor = blend_terms(base, moved, labels, mask, gain, ids)
    return blend(term, factor, squares, classes, class_total)


def solution(mesh):
    in_specs = (
        P("row", "node"),
        P("row", "cls"),
        P("cls"),
        P(("node", "row")),
        P(("node", "row")),
        P(("node", "row")),
        P(("node", "row"), None),
        P(("node", "row"), None, None),
        P(("node", "row")),
        P(("node", "row"), None, None, None),
        P("cls"),
    )
    out_specs = P("cls", ("node", "row"))
    return jax.shard_map(shards, mesh=mesh, in_specs=in_specs, out_specs=out_specs, check_vma=False)
```

```python
import jax
import jax.numpy as jnp
from jax import lax
from jax.experimental import pallas as pl
from jax.experimental.pallas import tpu as pltpu
from jax.sharding import PartitionSpec as P

HOPS = 2
TILE = 128
LO = 4
GROUP = 16
REST = 4
FIRST = 5

alpha_mix = 0.8
spread_eps = 1e-06

F32 = jnp.float32
BF16 = jnp.bfloat16
I32 = jnp.int32
VMEM = pl.BlockSpec(memory_space=pltpu.VMEM)
HBM = pl.BlockSpec(memory_space=pltpu.HBM)
SMEM = pl.BlockSpec(memory_space=pltpu.SMEM)


def iota(shape, dim):
    return lax.broadcasted_iota(I32, shape, dim)


def call(kernel, outs, ins, scratch=(), mb=12, flops=0, nbytes=0, name=None, where=None):
    return pl.pallas_call(
        kernel,
        out_shape=outs,
        in_specs=ins,
        out_specs=where or jax.tree.map(lambda _: VMEM, outs),
        scratch_shapes=list(scratch),
        compiler_params=pltpu.CompilerParams(vmem_limit_bytes=mb << 20),
        cost_estimate=pl.CostEstimate(flops=flops, bytes_accessed=nbytes, transcendentals=0),
        name=name,
    )


def in_hbm(*arrays):
    return [pltpu.with_memory_space_constraint(x, pltpu.HBM) for x in arrays]


def in_smem(x):
    return pltpu.with_memory_space_constraint(x, pltpu.SMEM)


def shape(dims, dtype):
    return jax.ShapeDtypeStruct(dims, dtype)


def up(value, step):
    return -(-value // step) * step


def step_between(a, b, count):
    assert count & (count - 1) == 0
    return a ^ b


def padded_weight(weight, padded):
    classes, depth = weight.shape
    weight = weight.astype(F32)
    return jnp.concatenate([weight, jnp.zeros((padded - classes, depth), F32)], axis=0).astype(BF16)


def node_block(ref, step, row_count, rows_here):
    at = step_between(lax.axis_index("row").astype(I32), step, row_count) * rows_here
    return ref.at[:, pl.ds(pl.multiple_of(at, TILE), rows_here)]


def partial_scores(features, weight, row_count, rows_here, padded):
    classes, depth = weight.shape
    steps = range(1, row_count)

    def kernel(f_hbm, w_hbm, *refs):
        outs = refs[: row_count - 1]
        f_ref, w_ref, sems = refs[row_count - 1 :]
        copies = [pltpu.make_async_copy(w_hbm, w_ref, sems.at[0])]
        for step in steps:
            source = node_block(f_hbm, step, row_count, rows_here)
            copies.append(pltpu.make_async_copy(source, f_ref.at[step - 1], sems.at[step]))
        for copy in copies:
            copy.start()
        copies[0].wait()
        w = padded_weight(w_ref[...], padded)
        for step in steps:
            copies[step].wait()
            score = jnp.dot(w, f_ref[step - 1], preferred_element_type=F32)
            outs[step - 1][...] = score.astype(BF16)

    out = shape((padded, rows_here), BF16)
    scratch = [
        pltpu.VMEM((row_count - 1, depth, rows_here), BF16),
        pltpu.VMEM((classes, depth), BF16),
        pltpu.SemaphoreType.DMA((row_count,)),
    ]
    return call(
        kernel, [out] * (row_count - 1), [HBM, HBM], scratch, name="partial_scores"
    )(*in_hbm(features, weight))


def slot_tables(pos, me, rows_here, part_count, capacity, aux_ref, hot_ref):
    tiles = rows_here // TILE
    share = capacity // LO
    columns = part_count * share
    block = pos // rows_here
    before = (iota((TILE, TILE), 0) < iota((TILE, TILE), 1)).astype(BF16)
    ones = jnp.ones((TILE, TILE), BF16)
    above = (iota((tiles, tiles), 1) < iota((tiles, tiles), 0)).astype(BF16)
    rank = jnp.zeros((tiles, TILE), F32)
    for d in range(part_count):
        member = block == d
        m = member.astype(F32).astype(BF16)
        inside = jnp.dot(m, before, preferred_element_type=F32)
        each = jnp.dot(m, ones, preferred_element_type=F32).astype(BF16)
        offset = jnp.dot(above, each, preferred_element_type=F32)
        rank = jnp.where(member, inside + offset, rank)
    rank = rank.astype(I32)
    low = rank // share
    column = step_between(block, me, part_count) * share + (rank - low * share)
    place = pos - block * rows_here
    power = place // TILE
    scale = jnp.ones((tiles, TILE), F32)
    for j in range(1, tiles):
        scale = jnp.where(power >= j, 2.0 * scale, scale)
    aux_ref[0] = low.astype(F32)
    aux_ref[1] = (place - power * TILE + TILE).astype(F32) * scale
    turned = jnp.concatenate([column, jnp.zeros((TILE - tiles, TILE), I32)], axis=0)
    turned = turned.astype(F32).T.astype(I32)
    across = iota((TILE, columns), 1)
    for j in range(tiles):
        hot = jnp.where(across == turned[:, j : j + 1], 1.0, 0.0)
        hot_ref[j * TILE : (j + 1) * TILE, :] = hot.astype(BF16)


def pair_tables(coords, live, here, counts, row_tiles, table_ref):
    node_count, row_count = counts
    slots = coords.shape[1]
    places = up(slots + row_tiles, 2 * REST)
    row = coords[0:1, :]
    column = coords[1:2, :]
    slot = iota((1, slots), 1)
    part = jnp.maximum(column - row_tiles, 0)
    part_node = part // row_count
    part_row = part - part_node * row_count
    node_step = step_between(part_node, here[0], node_count)
    row_step = step_between(part_row, here[1], row_count)
    before = (iota((slots, slots), 0) < iota((slots, slots), 1)).astype(BF16)
    ones = jnp.ones((slots, slots), BF16)
    above = (iota((row_tiles, row_tiles), 1) < iota((row_tiles, row_tiles), 0)).astype(BF16)
    line = iota((8, slots), 0)
    lane = iota((8, places), 1)
    for kind in range(3):
        if kind == 0:
            source = column
            wanted = column < row_tiles
        elif kind == 1:
            source = row_step
            wanted = (column >= row_tiles) & (node_step == 0)
        else:
            source = (node_step - 1) * row_count + row_step
            wanted = (column >= row_tiles) & (node_step > 0)
        member = (iota((row_tiles, slots), 0) == row) & (slot < live) & wanted
        m = jnp.where(member, 1.0, 0.0).astype(BF16)
        rank = jnp.dot(m, before, preferred_element_type=F32)
        number = jnp.dot(m, ones, preferred_element_type=F32).astype(I32)
        pairs = ((number + 1) // 2).astype(F32)
        first = jnp.dot(above, pairs.astype(BF16), preferred_element_type=F32)
        place = jnp.sum(jnp.where(member, 2.0 * first + rank + 1.0, 0.0), axis=0, keepdims=True)
        place = place.astype(I32) - 1
        hot = jnp.where(iota((places, slots), 0) == place, 1.0, 0.0).astype(BF16)
        values = jnp.where(
            line == 0, slot, jnp.where(line == 1, source + 1, jnp.where(line == 2, row, 0))
        )
        table = lax.dot_general(
            values.astype(F32).astype(BF16), hot, (((1,), (1,)), ((), ())), preferred_element_type=F32
        )
        total = jnp.sum(pairs, axis=0, keepdims=True).astype(I32)[:, :1]
        groups = total // GROUP
        rest = (total - groups * GROUP + REST - 1) // REST
        sizes = jnp.where(lane == 0, groups, rest)
        table_ref[kind] = jnp.where(iota((8, places), 0) == 3, sizes, table.astype(I32))


def own_tables(features, weight, positions, coords, live, rest, counts, padded, capacity, direct):
    node_count, row_count = counts
    classes, depth = weight.shape
    tiles = positions.shape[0]
    rows_here = tiles * TILE
    part_count = node_count * row_count
    columns = part_count * capacity // LO
    labels, mask, exports, bias, gain, adjacency = rest
    slots = adjacency.shape[0]

    def kernel(live_ref, *refs):
        node, row = lax.axis_index("node").astype(I32), lax.axis_index("row").astype(I32)
        f_hbm, w_hbm, p_hbm, c_hbm, l_hbm, m_hbm, e_hbm, b_hbm, g_hbm, a_hbm = refs[:10]
        score_ref, aux_ref, hot_ref, table_out, l_ref, m_ref, e_out, b_out, g_out, a_ref, i_out = refs[10:21]
        f_ref, w_ref, p_ref, c_ref, b_ref, g_ref, t_ref, e_ref, sems = refs[21:]
        source = node_block(f_hbm, 0, row_count, rows_here)
        pairs = [
            (p_hbm, p_ref),
            (c_hbm, c_ref),
            (b_hbm, b_ref),
            (g_hbm, g_ref),
            (e_hbm, e_ref),
            (w_hbm, w_ref),
            (source, f_ref),
            (l_hbm, l_ref),
            (m_hbm, m_ref),
            (a_hbm, a_ref),
        ]
        copies = [pltpu.make_async_copy(a, b, sems.at[i]) for i, (a, b) in enumerate(pairs)]
        for copy in copies:
            copy.start()
        for copy in copies[:5]:
            copy.wait()
        me = node * row_count + row if direct else 0
        slot_tables(p_ref[...], me, rows_here, part_count, capacity, aux_ref, hot_ref)
        pair_tables(c_ref[...], live_ref[0], (node, row), counts, tiles, t_ref)
        table_copy = pltpu.make_async_copy(t_ref, table_out, sems.at[10])
        table_copy.start()
        b_out[...] = jnp.broadcast_to(turned_column(b_ref[...], padded), (padded, TILE))
        g_out[...] = jnp.broadcast_to(turned_column(g_ref[...], padded), (padded, TILE))
        chosen = iota((rows_here, TILE), 0) == e_ref[...]
        e_out[...] = jnp.where(chosen, 1.0, 0.0).astype(BF16)
        line = iota((padded, TILE), 0)
        first = lax.axis_index("cls").astype(I32) * classes
        i_out[...] = jnp.where(line < classes, line + first, -1)
        table_copy.wait()
        for copy in copies[5:]:
            copy.wait()
        w = padded_weight(w_ref[...], padded)
        score_ref[...] = jnp.dot(w, f_ref[...], preferred_element_type=F32).astype(BF16)

    like = [shape(x.shape, x.dtype) for x in rest]
    outs = [
        shape((padded, rows_here), BF16),
        shape((2, tiles, TILE), F32),
        shape((rows_here, columns), BF16),
        pltpu.SMEM((3, 8, up(slots + tiles, 2 * REST)), I32),
        like[0],
        like[1],
        shape((rows_here, TILE), BF16),
        shape((padded, TILE), F32),
        shape((padded, TILE), F32),
        like[5],
        shape((padded, TILE), I32),
    ]
    scratch = [
        pltpu.VMEM((depth, rows_here), BF16),
        pltpu.VMEM((classes, depth), BF16),
        pltpu.VMEM(positions.shape, I32),
        pltpu.VMEM(coords.shape, I32),
        pltpu.VMEM(bias.shape, F32),
        pltpu.VMEM(gain.shape, F32),
        pltpu.VMEM(outs[3].shape, I32),
        pltpu.VMEM(exports.shape, I32),
        pltpu.SemaphoreType.DMA((11,)),
    ]
    where = [VMEM] * 3 + [SMEM] + [VMEM] * 7
    return call(kernel, outs, [SMEM] + [HBM] * 10, scratch, name="own_tables", where=where)(
        live, *in_hbm(features, weight, positions, coords, *rest)
    )


def turned_column(row, padded):
    row = jnp.concatenate([row, jnp.zeros((1, TILE - row.shape[1]), F32)], axis=1)
    return jnp.broadcast_to(row, (8, TILE)).T[:padded, 0:1]


def laid_block(laid, at, rows, padded):
    block = laid[:, at * TILE : (at + 1) * TILE]
    kept = jnp.concatenate([block[l * padded : l * padded + rows] for l in range(LO)], axis=0)
    return kept.astype(BF16)


def compact_scores(partials, bias, aux, hot, classes, padded):
    count = len(partials)
    rows_here = partials[0].shape[1]
    tiles = rows_here // TILE
    rows = classes + 1

    def kernel(*refs):
        parts = refs[:count]
        b_ref, aux_ref, hot_ref = refs[count : count + 3]
        outs, x_ref = refs[count + 3 : -1], refs[-1]
        bias_column = b_ref[...]
        row = iota((padded, TILE), 0)
        for j in range(tiles):
            cols = slice(j * TILE, (j + 1) * TILE)
            total = parts[0][:, cols].astype(F32)
            for other in parts[1:]:
                total = total + other[:, cols].astype(F32)
            value = (total + bias_column).astype(BF16).astype(F32)
            low = aux_ref[0, j : j + 1, :]
            value = jnp.where(row == classes, aux_ref[1, j : j + 1, :], value)
            for l in range(LO):
                x_ref[l * padded : (l + 1) * padded, cols] = jnp.where(low == l, value, 0.0).astype(BF16)
        laid = jnp.dot(x_ref[...], hot_ref[...], preferred_element_type=F32)
        for d, out in enumerate(outs):
            out[...] = laid_block(laid, d, rows, padded)

    return call(
        kernel,
        [shape((LO * rows, TILE), BF16)] * (hot.shape[1] // TILE),
        [VMEM] * (count + 3),
        [pltpu.VMEM((LO * padded, rows_here), BF16)],
        name="compact_scores",
    )(*partials, bias, aux, hot)


def placed(r_refs, x_ref, hot_ref, rows_here, classes, padded):
    rows = classes + 1
    high = rows_here // LO
    blocks = len(r_refs)
    width = LO * rows
    pick = iota((8, width), 1) - iota((8, width), 0) * rows == classes
    pick = jnp.where(pick & (iota((8, width), 0) < LO), 1.0, 0.0).astype(BF16)
    held = [jnp.dot(pick, ref[...], preferred_element_type=F32) for ref in r_refs]
    held = jnp.concatenate(held, axis=0)
    power = jnp.zeros(held.shape, I32)
    scale = jnp.ones(held.shape, F32)
    for j in range(1, rows_here // TILE):
        above = held >= float(TILE << j)
        power = jnp.where(above, j, power)
        scale = jnp.where(above, 0.5**j, scale)
    code = jnp.where(held > 0.0, power * TILE + (held * scale).astype(I32) - TILE, -1)
    group = jnp.where(code < 0, -1, code // high)
    inner = (code & (high - 1)).astype(F32)
    rest = jnp.zeros((TILE - 8 * blocks, TILE), F32)
    turned = jnp.concatenate([inner, rest], axis=0).T.astype(I32)
    across = iota((TILE, high), 1)
    tail = jnp.zeros((padded - rows, TILE), F32)
    for s in range(blocks):
        block = r_refs[s][...].astype(F32)
        for l in range(LO):
            at = (s * LO + l) * TILE
            lane = s * 8 + l
            hot = jnp.where(across == turned[:, lane : lane + 1], 1.0, 0.0)
            hot_ref[at : at + TILE, :] = hot.astype(BF16)
            value = jnp.concatenate([block[l * rows : (l + 1) * rows], tail], axis=0)
            mine = group[lane : lane + 1, :]
            for q in range(LO):
                x_ref[q * padded : (q + 1) * padded, at : at + TILE] = jnp.where(
                    mine == q, value, 0.0
                ).astype(BF16)
    return jnp.dot(x_ref[...], hot_ref[...], preferred_element_type=F32)


def place_scratch(blocks, rows_here, padded):
    width = blocks * LO * TILE
    return [pltpu.VMEM((LO * padded, width), BF16), pltpu.VMEM((width, rows_here // LO), BF16)]


def place_first(received, rows_here, classes, padded):
    blocks = len(received)

    def kernel(*refs):
        out_ref, x_ref, hot_ref = refs[blocks:]
        out_ref[...] = placed(refs[:blocks], x_ref, hot_ref, rows_here, classes, padded)

    flops = 2 * LO * padded * rows_here * blocks * TILE
    return call(
        kernel,
        [shape((LO * padded, rows_here // LO), F32)],
        [VMEM] * blocks,
        place_scratch(blocks, rows_here, padded),
        flops=flops,
        nbytes=4 * LO * padded * rows_here // LO,
        name="place_first",
    )(*received)[0]


def place_scores(first, received, rows_here, classes, padded):
    blocks = len(received)
    tiles = rows_here // TILE

    def kernel(*refs):
        first_ref = refs[0]
        raised_ref, total_ref, x_ref, hot_ref = refs[1 + blocks :]
        logits = placed(refs[1 : 1 + blocks], x_ref, hot_ref, rows_here, classes, padded)
        logits = logits + first_ref[...]
        row = iota((padded, TILE), 0)
        for i in range(tiles):
            q, c = divmod(i, tiles // LO)
            part = logits[q * padded : (q + 1) * padded, c * TILE : (c + 1) * TILE]
            raised = jnp.where(row < classes, jnp.exp(part), 0.0)
            raised_ref[i] = raised
            total_ref[i : i + 1, :] = jnp.sum(raised, axis=0, keepdims=True)

    return call(
        kernel,
        [shape((tiles, padded, TILE), F32), shape((tiles, TILE), F32)],
        [VMEM] * (1 + blocks),
        place_scratch(blocks, rows_here, padded),
        name="place_scores",
    )(first, *received)


def exported_columns(moved_tiles, chosen):
    source = jnp.concatenate(moved_tiles, axis=1)
    return jnp.dot(source, chosen, preferred_element_type=F32).astype(BF16)


def start_residuals(raised, totals, labels, mask, exports, ids):
    tiles, padded, _ = raised.shape
    count = len(totals)

    def kernel(ids_ref, raised_ref, *refs):
        total_refs = refs[:count]
        label_ref, mask_ref, export_ref, base_ref, start_ref, moved_ref, out_ref = refs[count:]
        total = total_refs[0][...]
        for other in total_refs[1:]:
            total = total + other[...]
        ids = ids_ref[...]
        moved = []
        for i in range(tiles):
            base = raised_ref[i] / total[i : i + 1, :]
            truth = jnp.where(ids == label_ref[i : i + 1, :], 1.0, 0.0)
            start = mask_ref[i : i + 1, :].astype(F32) * (truth - base)
            base_ref[i] = base
            start_ref[i] = start
            moved.append(start.astype(BF16))
            moved_ref[i] = moved[-1]
        out_ref[...] = exported_columns(moved, export_ref[...])

    full = shape((tiles, padded, TILE), F32)
    outs = [full, full, shape((tiles, padded, TILE), BF16), shape((padded, TILE), BF16)]
    return call(kernel, outs, [VMEM] * (count + 5), name="start_residuals")(
        ids, raised, *totals, labels, mask, exports
    )


def pair_products(table_ref, kind, s_ref, a_ref, acc_ref):
    acc_ref[...] = jnp.zeros_like(acc_ref)

    def product(k):
        slots = [table_ref[kind, 0, k], table_ref[kind, 0, k + 1]]
        sources = [table_ref[kind, 1, k], table_ref[kind, 1, k + 1]]
        left = jnp.concatenate([s_ref[j] for j in sources], axis=1)
        right = jnp.concatenate([a_ref[t] for t in slots], axis=1)
        acc_ref[table_ref[kind, 2, k]] += lax.dot_general(
            left, right, (((1,), (1,)), ((), ())), preferred_element_type=F32
        )

    def several(first, count):
        def step(group, carry):
            for u in range(count):
                product(2 * (first + group * count + u))
            return carry

        return step

    groups = table_ref[kind, 3, 0]
    lax.fori_loop(0, groups, several(0, GROUP), 0)
    lax.fori_loop(0, table_ref[kind, 3, 1], several(groups * GROUP, REST), 0)


def own_products(table, moved, adjacency):
    tiles, padded, _ = moved.shape

    def kernel(t_ref, moved_ref, a_ref, acc_ref, s_ref):
        s_ref[0] = jnp.zeros((padded, TILE), BF16)
        for i in range(tiles):
            s_ref[1 + i] = moved_ref[i]
        pair_products(t_ref, 0, s_ref, a_ref, acc_ref)

    return call(
        kernel,
        shape((tiles, padded, TILE), F32),
        [SMEM, VMEM, VMEM],
        [pltpu.VMEM((1 + tiles, padded, TILE), BF16)],
        name="own_products",
    )(in_smem(table), moved, adjacency)


def near_products(table, group, adjacency, own):
    tiles, padded, _ = own.shape
    count = group.shape[0]

    def kernel(t_ref, group_ref, a_ref, own_ref, out_ref, s_ref):
        s_ref[0] = jnp.zeros((padded, TILE), BF16)
        for k in range(count):
            s_ref[1 + k] = group_ref[k]
        pair_products(t_ref, 1, s_ref, a_ref, out_ref)
        out_ref[...] += own_ref[...]

    return call(
        kernel,
        shape((tiles, padded, TILE), F32),
        [SMEM, VMEM, VMEM, VMEM],
        [pltpu.VMEM((1 + count, padded, TILE), BF16)],
        name="near_products",
    )(in_smem(table), group, adjacency, own)


def hop(table, boundary, adjacency, own, start, exports, last):
    tiles, padded, _ = start.shape
    count = len(boundary)
    sources = sum(b.shape[0] for b in boundary)

    def kernel(*refs):
        t_ref = refs[0]
        boundary_refs = refs[1 : 1 + count]
        a_ref, own_ref, start_ref, export_ref, first_out, second_out, s_ref, acc_ref = refs[1 + count :]
        s_ref[0] = jnp.zeros((padded, TILE), BF16)
        at = 1
        for ref in boundary_refs:
            for k in range(ref.shape[0]):
                s_ref[at] = ref[k]
                at += 1
        pair_products(t_ref, 2, s_ref, a_ref, acc_ref)
        moved_out = []
        for i in range(tiles):
            spread = own_ref[i] + acc_ref[i]
            residual = (1.0 - alpha_mix) * start_ref[i] + alpha_mix * spread
            if last:
                first_out[i] = residual
                second_out[i : i + 1, :] = jnp.sum(residual * residual, axis=0, keepdims=True)
            else:
                moved_out.append(residual.astype(BF16))
                first_out[i] = moved_out[-1]
        if not last:
            second_out[...] = exported_columns(moved_out, export_ref[...])

    if last:
        outs = [shape((tiles, padded, TILE), F32), shape((tiles, TILE), F32)]
    else:
        outs = [shape((tiles, padded, TILE), BF16), shape((padded, TILE), BF16)]
    return call(
        kernel,
        outs,
        [SMEM] + [VMEM] * (count + 4),
        [pltpu.VMEM((1 + sources, padded, TILE), BF16), pltpu.VMEM((tiles, padded, TILE), F32)],
        name="hop",
    )(in_smem(table), *boundary, adjacency, own, start, exports)


def blend_terms(base, residual, labels, mask, gain, ids):
    tiles, padded, _ = base.shape

    def kernel(ids_ref, base_ref, residual_ref, label_ref, mask_ref, gain_ref, term_ref, factor_ref):
        ids = ids_ref[...]
        gains = gain_ref[...]
        for i in range(tiles):
            truth = jnp.where(ids == label_ref[i : i + 1, :], 1.0, 0.0)
            trained = mask_ref[i : i + 1, :] == 1
            term_ref[i] = jnp.where(trained, truth, base_ref[i])
            factor_ref[i] = jnp.where(trained, 0.0, gains * residual_ref[i])

    full = shape((tiles, padded, TILE), F32)
    return call(kernel, [full, full], [VMEM] * 6, name="blend_terms")(
        ids, base, residual, labels, mask, gain
    )


def blend(term, factor, squares, classes, class_total):
    tiles, padded, _ = term.shape
    count = len(squares)
    cuts = 4
    each = tiles // cuts

    def kernel(term_ref, factor_ref, *refs):
        square_refs = refs[:count]
        out_hbm, out_ref, sems = refs[count:]
        total = square_refs[0][...]
        for other in square_refs[1:]:
            total = total + other[...]
        inverse = lax.rsqrt(total / float(class_total) + spread_eps)
        copies = []
        for cut in range(cuts):
            for i in range(cut * each, (cut + 1) * each):
                blended = term_ref[i] + factor_ref[i] * inverse[i : i + 1, :]
                out_ref[:, i * TILE : (i + 1) * TILE] = blended[:classes]
            cols = pl.ds(cut * each * TILE, each * TILE)
            copy = pltpu.make_async_copy(out_ref.at[:, cols], out_hbm.at[:, cols], sems.at[cut])
            copy.start()
            copies.append(copy)
        for copy in copies:
            copy.wait()

    return call(
        kernel,
        shape((classes, tiles * TILE), F32),
        [VMEM] * (count + 2),
        [pltpu.VMEM((classes, tiles * TILE), F32), pltpu.SemaphoreType.DMA((cuts,))],
        name="blend",
        where=HBM,
    )(term, factor, *squares)


def exchanged(value, axis, count, step):
    return lax.ppermute(value, axis, [(i, step_between(i, step, count)) for i in range(count)])


def from_all(value, axis):
    count = lax.axis_size(axis)
    steps = sorted(range(1, count), key=lambda step: (step + 1) % 4 if axis == "node" else step)
    got = {step: exchanged(value, axis, count, step) for step in steps}
    return [value] + [got[step] for step in range(1, count)]


def shards(
    features,
    class_weight,
    class_bias,
    part_position,
    labels,
    train_mask,
    export_rows,
    tile_coords,
    tile_count,
    adjacency,
    corr_gain,
):
    node_count = lax.axis_size("node")
    row_count = lax.axis_size("row")
    part_count = node_count * row_count
    rows_here = part_position.shape[0]
    classes = class_bias.shape[0]
    class_total = classes * lax.axis_size("cls")
    padded = up(classes + 1, 16)
    tiles = rows_here // TILE
    capacity = 2 * rows_here // part_count
    counts = (node_count, row_count)
    labels = labels.reshape(tiles, TILE)
    mask = train_mask.reshape(tiles, TILE)
    weight = class_weight.T
    share = capacity // LO
    direct = share == TILE
    parts = partial_scores(features, weight, row_count, rows_here, padded)
    partials = [
        exchanged(parts[step - 1], "row", row_count, step) for step in range(1, row_count)
    ]
    rest = (labels, mask, export_rows, class_bias[None], corr_gain[None], adjacency[0])
    score, aux, hot, table, labels, mask, exports, bias, gain, adjacency, ids = own_tables(
        features,
        weight,
        part_position.reshape(tiles, TILE),
        tile_coords[0],
        tile_count,
        rest,
        counts,
        padded,
        capacity,
        direct,
    )
    sending = compact_scores([score] + partials, bias, aux, hot, classes, padded)
    if direct:
        axes = ("node", "row")
        received = [sending[0]] + [
            exchanged(sending[step], axes, part_count, step) for step in ([2, 7, 6, 5, 4, 3, 1] if part_count == 8 else range(1, part_count))
        ]
    else:
        blocks, width = len(sending), sending[0].shape[0]
        sent = jnp.stack(sending)
        sent = sent.reshape(blocks, width, TILE // share, share).transpose(0, 2, 1, 3)
        sent = sent.reshape(part_count, width, share)
        got = lax.all_to_all(sent, ("node", "row"), split_axis=0, concat_axis=0, tiled=True)
        got = got.reshape(blocks, TILE // share, width, share).transpose(0, 2, 1, 3)
        got = got.reshape(blocks, width, TILE)
        received = [got[s] for s in range(blocks)]
    first = place_first(received[:FIRST], rows_here, classes, padded)
    raised, total = place_scores(first, received[FIRST:], rows_here, classes, padded)
    totals = from_all(total, "cls")
    base, start, moved, out = start_residuals(
        raised, totals, labels, mask, exports, ids
    )
    for index in range(HOPS):
        group = jnp.stack(from_all(out, "row"))
        own = own_products(table, moved, adjacency)
        group, own = lax.optimization_barrier((group, own))
        _, *boundary = from_all(group, "node")
        own = near_products(table, group, adjacency, own)
        moved, out = hop(
            table, boundary, adjacency, own, start, exports, index == HOPS - 1
        )
    squares = from_all(out, "cls")
    term, factor = blend_terms(base, moved, labels, mask, gain, ids)
    return blend(term, factor, squares, classes, class_total)


def solution(mesh):
    in_specs = (
        P("row", "node"),
        P("row", "cls"),
        P("cls"),
        P(("node", "row")),
        P(("node", "row")),
        P(("node", "row")),
        P(("node", "row"), None),
        P(("node", "row"), None, None),
        P(("node", "row")),
        P(("node", "row"), None, None, None),
        P("cls"),
    )
    out_specs = P("cls", ("node", "row"))
    return jax.shard_map(shards, mesh=mesh, in_specs=in_specs, out_specs=out_specs, check_vma=False)
```

```python
import jax
import jax.numpy as jnp
from jax import lax
from jax.experimental import pallas as pl
from jax.experimental.pallas import tpu as pltpu
from jax.sharding import PartitionSpec as P

HOPS = 2
TILE = 128
LO = 4
GROUP = 16
REST = 4
FIRST = 5

alpha_mix = 0.8
spread_eps = 1e-06

F32 = jnp.float32
BF16 = jnp.bfloat16
I32 = jnp.int32
VMEM = pl.BlockSpec(memory_space=pltpu.VMEM)
HBM = pl.BlockSpec(memory_space=pltpu.HBM)
SMEM = pl.BlockSpec(memory_space=pltpu.SMEM)


def iota(shape, dim):
    return lax.broadcasted_iota(I32, shape, dim)


def call(kernel, outs, ins, scratch=(), mb=12, flops=0, nbytes=0, name=None, where=None):
    return pl.pallas_call(
        kernel,
        out_shape=outs,
        in_specs=ins,
        out_specs=where or jax.tree.map(lambda _: VMEM, outs),
        scratch_shapes=list(scratch),
        compiler_params=pltpu.CompilerParams(vmem_limit_bytes=mb << 20),
        cost_estimate=pl.CostEstimate(flops=flops, bytes_accessed=nbytes, transcendentals=0),
        name=name,
    )


def in_hbm(*arrays):
    return [pltpu.with_memory_space_constraint(x, pltpu.HBM) for x in arrays]


def in_smem(x):
    return pltpu.with_memory_space_constraint(x, pltpu.SMEM)


def shape(dims, dtype):
    return jax.ShapeDtypeStruct(dims, dtype)


def up(value, step):
    return -(-value // step) * step


def step_between(a, b, count):
    assert count & (count - 1) == 0
    return a ^ b


def padded_weight(weight, padded):
    classes, depth = weight.shape
    weight = weight.astype(F32)
    return jnp.concatenate([weight, jnp.zeros((padded - classes, depth), F32)], axis=0).astype(BF16)


def node_block(ref, step, row_count, rows_here):
    at = step_between(lax.axis_index("row").astype(I32), step, row_count) * rows_here
    return ref.at[:, pl.ds(pl.multiple_of(at, TILE), rows_here)]


def partial_scores(features, weight, row_count, rows_here, padded):
    classes, depth = weight.shape
    steps = range(1, row_count)

    def kernel(f_hbm, w_hbm, *refs):
        outs = refs[: row_count - 1]
        f_ref, w_ref, sems = refs[row_count - 1 :]
        copies = [pltpu.make_async_copy(w_hbm, w_ref, sems.at[0])]
        for step in steps:
            source = node_block(f_hbm, step, row_count, rows_here)
            copies.append(pltpu.make_async_copy(source, f_ref.at[step - 1], sems.at[step]))
        for copy in copies:
            copy.start()
        copies[0].wait()
        w = padded_weight(w_ref[...], padded)
        for step in steps:
            copies[step].wait()
            score = jnp.dot(w, f_ref[step - 1], preferred_element_type=F32)
            outs[step - 1][...] = score.astype(BF16)

    out = shape((padded, rows_here), BF16)
    scratch = [
        pltpu.VMEM((row_count - 1, depth, rows_here), BF16),
        pltpu.VMEM((classes, depth), BF16),
        pltpu.SemaphoreType.DMA((row_count,)),
    ]
    return call(
        kernel, [out] * (row_count - 1), [HBM, HBM], scratch, name="partial_scores"
    )(*in_hbm(features, weight))


def slot_tables(pos, me, rows_here, part_count, capacity, aux_ref, hot_ref):
    tiles = rows_here // TILE
    share = capacity // LO
    columns = part_count * share
    block = pos // rows_here
    before = (iota((TILE, TILE), 0) < iota((TILE, TILE), 1)).astype(BF16)
    ones = jnp.ones((TILE, TILE), BF16)
    above = (iota((tiles, tiles), 1) < iota((tiles, tiles), 0)).astype(BF16)
    rank = jnp.zeros((tiles, TILE), F32)
    for d in range(part_count):
        member = block == d
        m = member.astype(F32).astype(BF16)
        inside = jnp.dot(m, before, preferred_element_type=F32)
        each = jnp.dot(m, ones, preferred_element_type=F32).astype(BF16)
        offset = jnp.dot(above, each, preferred_element_type=F32)
        rank = jnp.where(member, inside + offset, rank)
    rank = rank.astype(I32)
    low = rank // share
    column = step_between(block, me, part_count) * share + (rank - low * share)
    place = pos - block * rows_here
    power = place // TILE
    scale = jnp.ones((tiles, TILE), F32)
    for j in range(1, tiles):
        scale = jnp.where(power >= j, 2.0 * scale, scale)
    aux_ref[0] = low.astype(F32)
    aux_ref[1] = (place - power * TILE + TILE).astype(F32) * scale
    turned = jnp.concatenate([column, jnp.zeros((TILE - tiles, TILE), I32)], axis=0)
    turned = turned.astype(F32).T.astype(I32)
    across = iota((TILE, columns), 1)
    for j in range(tiles):
        hot = jnp.where(across == turned[:, j : j + 1], 1.0, 0.0)
        hot_ref[j * TILE : (j + 1) * TILE, :] = hot.astype(BF16)


def pair_tables(coords, live, here, counts, row_tiles, table_ref):
    node_count, row_count = counts
    slots = coords.shape[1]
    places = up(slots + row_tiles, 2 * REST)
    row = coords[0:1, :]
    column = coords[1:2, :]
    slot = iota((1, slots), 1)
    part = jnp.maximum(column - row_tiles, 0)
    part_node = part // row_count
    part_row = part - part_node * row_count
    node_step = step_between(part_node, here[0], node_count)
    row_step = step_between(part_row, here[1], row_count)
    before = (iota((slots, slots), 0) < iota((slots, slots), 1)).astype(BF16)
    ones = jnp.ones((slots, slots), BF16)
    above = (iota((row_tiles, row_tiles), 1) < iota((row_tiles, row_tiles), 0)).astype(BF16)
    line = iota((8, slots), 0)
    lane = iota((8, places), 1)
    for kind in range(3):
        if kind == 0:
            source = column
            wanted = column < row_tiles
        elif kind == 1:
            source = row_step
            wanted = (column >= row_tiles) & (node_step == 0)
        else:
            source = (node_step - 1) * row_count + row_step
            wanted = (column >= row_tiles) & (node_step > 0)
        member = (iota((row_tiles, slots), 0) == row) & (slot < live) & wanted
        m = jnp.where(member, 1.0, 0.0).astype(BF16)
        rank = jnp.dot(m, before, preferred_element_type=F32)
        number = jnp.dot(m, ones, preferred_element_type=F32).astype(I32)
        pairs = ((number + 1) // 2).astype(F32)
        first = jnp.dot(above, pairs.astype(BF16), preferred_element_type=F32)
        place = jnp.sum(jnp.where(member, 2.0 * first + rank + 1.0, 0.0), axis=0, keepdims=True)
        place = place.astype(I32) - 1
        hot = jnp.where(iota((places, slots), 0) == place, 1.0, 0.0).astype(BF16)
        values = jnp.where(
            line == 0, slot, jnp.where(line == 1, source + 1, jnp.where(line == 2, row, 0))
        )
        table = lax.dot_general(
            values.astype(F32).astype(BF16), hot, (((1,), (1,)), ((), ())), preferred_element_type=F32
        )
        total = jnp.sum(pairs, axis=0, keepdims=True).astype(I32)[:, :1]
        groups = total // GROUP
        rest = (total - groups * GROUP + REST - 1) // REST
        sizes = jnp.where(lane == 0, groups, rest)
        table_ref[kind] = jnp.where(iota((8, places), 0) == 3, sizes, table.astype(I32))


def own_tables(features, weight, positions, coords, live, rest, counts, padded, capacity, direct):
    node_count, row_count = counts
    classes, depth = weight.shape
    tiles = positions.shape[0]
    rows_here = tiles * TILE
    part_count = node_count * row_count
    columns = part_count * capacity // LO
    labels, mask, exports, bias, gain, adjacency = rest
    slots = adjacency.shape[0]

    def kernel(live_ref, *refs):
        node, row = lax.axis_index("node").astype(I32), lax.axis_index("row").astype(I32)
        f_hbm, w_hbm, p_hbm, c_hbm, l_hbm, m_hbm, e_hbm, b_hbm, g_hbm, a_hbm = refs[:10]
        score_ref, aux_ref, hot_ref, table_out, l_ref, m_ref, e_out, b_out, g_out, a_ref, i_out = refs[10:21]
        f_ref, w_ref, p_ref, c_ref, b_ref, g_ref, t_ref, e_ref, sems = refs[21:]
        source = node_block(f_hbm, 0, row_count, rows_here)
        pairs = [
            (p_hbm, p_ref),
            (c_hbm, c_ref),
            (b_hbm, b_ref),
            (g_hbm, g_ref),
            (e_hbm, e_ref),
            (w_hbm, w_ref),
            (source, f_ref),
            (l_hbm, l_ref),
            (m_hbm, m_ref),
            (a_hbm, a_ref),
        ]
        copies = [pltpu.make_async_copy(a, b, sems.at[i]) for i, (a, b) in enumerate(pairs)]
        for copy in copies:
            copy.start()
        for copy in copies[:5]:
            copy.wait()
        me = node * row_count + row if direct else 0
        slot_tables(p_ref[...], me, rows_here, part_count, capacity, aux_ref, hot_ref)
        pair_tables(c_ref[...], live_ref[0], (node, row), counts, tiles, t_ref)
        table_copy = pltpu.make_async_copy(t_ref, table_out, sems.at[10])
        table_copy.start()
        b_out[...] = jnp.broadcast_to(turned_column(b_ref[...], padded), (padded, TILE))
        g_out[...] = jnp.broadcast_to(turned_column(g_ref[...], padded), (padded, TILE))
        chosen = iota((rows_here, TILE), 0) == e_ref[...]
        e_out[...] = jnp.where(chosen, 1.0, 0.0).astype(BF16)
        line = iota((padded, TILE), 0)
        first = lax.axis_index("cls").astype(I32) * classes
        i_out[...] = jnp.where(line < classes, line + first, -1)
        table_copy.wait()
        for copy in copies[5:]:
            copy.wait()
        w = padded_weight(w_ref[...], padded)
        score_ref[...] = jnp.dot(w, f_ref[...], preferred_element_type=F32).astype(BF16)

    like = [shape(x.shape, x.dtype) for x in rest]
    outs = [
        shape((padded, rows_here), BF16),
        shape((2, tiles, TILE), F32),
        shape((rows_here, columns), BF16),
        pltpu.SMEM((3, 8, up(slots + tiles, 2 * REST)), I32),
        like[0],
        like[1],
        shape((rows_here, TILE), BF16),
        shape((padded, TILE), F32),
        shape((padded, TILE), F32),
        like[5],
        shape((padded, TILE), I32),
    ]
    scratch = [
        pltpu.VMEM((depth, rows_here), BF16),
        pltpu.VMEM((classes, depth), BF16),
        pltpu.VMEM(positions.shape, I32),
        pltpu.VMEM(coords.shape, I32),
        pltpu.VMEM(bias.shape, F32),
        pltpu.VMEM(gain.shape, F32),
        pltpu.VMEM(outs[3].shape, I32),
        pltpu.VMEM(exports.shape, I32),
        pltpu.SemaphoreType.DMA((11,)),
    ]
    where = [VMEM] * 3 + [SMEM] + [VMEM] * 7
    return call(kernel, outs, [SMEM] + [HBM] * 10, scratch, name="own_tables", where=where)(
        live, *in_hbm(features, weight, positions, coords, *rest)
    )


def turned_column(row, padded):
    row = jnp.concatenate([row, jnp.zeros((1, TILE - row.shape[1]), F32)], axis=1)
    return jnp.broadcast_to(row, (8, TILE)).T[:padded, 0:1]


def laid_block(laid, at, rows, padded):
    block = laid[:, at * TILE : (at + 1) * TILE]
    kept = jnp.concatenate([block[l * padded : l * padded + rows] for l in range(LO)], axis=0)
    return kept.astype(BF16)


def compact_scores(partials, bias, aux, hot, classes, padded):
    count = len(partials)
    rows_here = partials[0].shape[1]
    tiles = rows_here // TILE
    rows = classes + 1

    def kernel(*refs):
        parts = refs[:count]
        b_ref, aux_ref, hot_ref = refs[count : count + 3]
        outs, x_ref = refs[count + 3 : -1], refs[-1]
        bias_column = b_ref[...]
        row = iota((padded, TILE), 0)
        for j in range(tiles):
            cols = slice(j * TILE, (j + 1) * TILE)
            total = parts[0][:, cols].astype(F32)
            for other in parts[1:]:
                total = total + other[:, cols].astype(F32)
            value = (total + bias_column).astype(BF16).astype(F32)
            low = aux_ref[0, j : j + 1, :]
            value = jnp.where(row == classes, aux_ref[1, j : j + 1, :], value)
            for l in range(LO):
                x_ref[l * padded : (l + 1) * padded, cols] = jnp.where(low == l, value, 0.0).astype(BF16)
        laid = jnp.dot(x_ref[...], hot_ref[...], preferred_element_type=F32)
        for d, out in enumerate(outs):
            out[...] = laid_block(laid, d, rows, padded)

    return call(
        kernel,
        [shape((LO * rows, TILE), BF16)] * (hot.shape[1] // TILE),
        [VMEM] * (count + 3),
        [pltpu.VMEM((LO * padded, rows_here), BF16)],
        name="compact_scores",
    )(*partials, bias, aux, hot)


def placed(r_refs, x_ref, hot_ref, rows_here, classes, padded):
    rows = classes + 1
    high = rows_here // LO
    blocks = len(r_refs)
    width = LO * rows
    pick = iota((8, width), 1) - iota((8, width), 0) * rows == classes
    pick = jnp.where(pick & (iota((8, width), 0) < LO), 1.0, 0.0).astype(BF16)
    held = [jnp.dot(pick, ref[...], preferred_element_type=F32) for ref in r_refs]
    held = jnp.concatenate(held, axis=0)
    power = jnp.zeros(held.shape, I32)
    scale = jnp.ones(held.shape, F32)
    for j in range(1, rows_here // TILE):
        above = held >= float(TILE << j)
        power = jnp.where(above, j, power)
        scale = jnp.where(above, 0.5**j, scale)
    code = jnp.where(held > 0.0, power * TILE + (held * scale).astype(I32) - TILE, -1)
    group = jnp.where(code < 0, -1, code // high)
    inner = (code & (high - 1)).astype(F32)
    rest = jnp.zeros((TILE - 8 * blocks, TILE), F32)
    turned = jnp.concatenate([inner, rest], axis=0).T.astype(I32)
    across = iota((TILE, high), 1)
    tail = jnp.zeros((padded - rows, TILE), F32)
    for s in range(blocks):
        block = r_refs[s][...].astype(F32)
        for l in range(LO):
            at = (s * LO + l) * TILE
            lane = s * 8 + l
            hot = jnp.where(across == turned[:, lane : lane + 1], 1.0, 0.0)
            hot_ref[at : at + TILE, :] = hot.astype(BF16)
            value = jnp.concatenate([block[l * rows : (l + 1) * rows], tail], axis=0)
            mine = group[lane : lane + 1, :]
            for q in range(LO):
                x_ref[q * padded : (q + 1) * padded, at : at + TILE] = jnp.where(
                    mine == q, value, 0.0
                ).astype(BF16)
    return jnp.dot(x_ref[...], hot_ref[...], preferred_element_type=F32)


def place_scratch(blocks, rows_here, padded):
    width = blocks * LO * TILE
    return [pltpu.VMEM((LO * padded, width), BF16), pltpu.VMEM((width, rows_here // LO), BF16)]


def place_first(received, rows_here, classes, padded):
    blocks = len(received)

    def kernel(*refs):
        out_ref, x_ref, hot_ref = refs[blocks:]
        out_ref[...] = placed(refs[:blocks], x_ref, hot_ref, rows_here, classes, padded)

    flops = 2 * LO * padded * rows_here * blocks * TILE
    return call(
        kernel,
        [shape((LO * padded, rows_here // LO), F32)],
        [VMEM] * blocks,
        place_scratch(blocks, rows_here, padded),
        flops=flops,
        nbytes=4 * LO * padded * rows_here // LO,
        name="place_first",
    )(*received)[0]


def place_scores(first, received, rows_here, classes, padded):
    blocks = len(received)
    tiles = rows_here // TILE

    def kernel(*refs):
        first_ref = refs[0]
        raised_ref, total_ref, x_ref, hot_ref = refs[1 + blocks :]
        logits = placed(refs[1 : 1 + blocks], x_ref, hot_ref, rows_here, classes, padded)
        logits = logits + first_ref[...]
        row = iota((padded, TILE), 0)
        for i in range(tiles):
            q, c = divmod(i, tiles // LO)
            part = logits[q * padded : (q + 1) * padded, c * TILE : (c + 1) * TILE]
            raised = jnp.where(row < classes, jnp.exp(part), 0.0)
            raised_ref[i] = raised
            total_ref[i : i + 1, :] = jnp.sum(raised, axis=0, keepdims=True)

    return call(
        kernel,
        [shape((tiles, padded, TILE), F32), shape((tiles, TILE), F32)],
        [VMEM] * (1 + blocks),
        place_scratch(blocks, rows_here, padded),
        name="place_scores",
    )(first, *received)


def exported_columns(moved_tiles, chosen):
    source = jnp.concatenate(moved_tiles, axis=1)
    return jnp.dot(source, chosen, preferred_element_type=F32).astype(BF16)


def base_and_start(raised, total, label, mask, ids):
    base = raised / total
    truth = jnp.where(ids == label, 1.0, 0.0)
    return base, mask.astype(F32) * (truth - base)


def first_moved(raised, totals, labels, mask, exports, ids):
    tiles, padded, _ = raised.shape
    count = len(totals)

    def kernel(ids_ref, raised_ref, *refs):
        total_refs = refs[:count]
        label_ref, mask_ref, export_ref, moved_ref, out_ref, total_ref = refs[count:]
        total = total_refs[0][...]
        for other in total_refs[1:]:
            total = total + other[...]
        total_ref[...] = total
        moved = []
        for i in range(tiles):
            line = slice(i, i + 1)
            _, start = base_and_start(
                raised_ref[i], total[line], label_ref[line, :], mask_ref[line, :], ids_ref[...]
            )
            moved.append(start.astype(BF16))
            moved_ref[i] = moved[-1]
        out_ref[...] = exported_columns(moved, export_ref[...])

    outs = [
        shape((tiles, padded, TILE), BF16),
        shape((padded, TILE), BF16),
        shape((tiles, TILE), F32),
    ]
    return call(kernel, outs, [VMEM] * (count + 5), name="first_moved")(
        ids, raised, *totals, labels, mask, exports
    )


def start_residuals(raised, total, labels, mask, ids):
    tiles, padded, _ = raised.shape

    def kernel(ids_ref, raised_ref, total_ref, label_ref, mask_ref, base_ref, start_ref):
        for i in range(tiles):
            line = slice(i, i + 1)
            base_ref[i], start_ref[i] = base_and_start(
                raised_ref[i], total_ref[line, :], label_ref[line, :], mask_ref[line, :], ids_ref[...]
            )

    full = shape((tiles, padded, TILE), F32)
    return call(kernel, [full, full], [VMEM] * 5, name="start_residuals")(
        ids, raised, total, labels, mask
    )


def pair_products(table_ref, kind, s_ref, a_ref, acc_ref):
    acc_ref[...] = jnp.zeros_like(acc_ref)

    def product(k):
        slots = [table_ref[kind, 0, k], table_ref[kind, 0, k + 1]]
        sources = [table_ref[kind, 1, k], table_ref[kind, 1, k + 1]]
        left = jnp.concatenate([s_ref[j] for j in sources], axis=1)
        right = jnp.concatenate([a_ref[t] for t in slots], axis=1)
        acc_ref[table_ref[kind, 2, k]] += lax.dot_general(
            left, right, (((1,), (1,)), ((), ())), preferred_element_type=F32
        )

    def several(first, count):
        def step(group, carry):
            for u in range(count):
                product(2 * (first + group * count + u))
            return carry

        return step

    groups = table_ref[kind, 3, 0]
    lax.fori_loop(0, groups, several(0, GROUP), 0)
    lax.fori_loop(0, table_ref[kind, 3, 1], several(groups * GROUP, REST), 0)


def own_products(table, moved, adjacency):
    tiles, padded, _ = moved.shape

    def kernel(t_ref, moved_ref, a_ref, acc_ref, s_ref):
        s_ref[0] = jnp.zeros((padded, TILE), BF16)
        for i in range(tiles):
            s_ref[1 + i] = moved_ref[i]
        pair_products(t_ref, 0, s_ref, a_ref, acc_ref)

    return call(
        kernel,
        shape((tiles, padded, TILE), F32),
        [SMEM, VMEM, VMEM],
        [pltpu.VMEM((1 + tiles, padded, TILE), BF16)],
        name="own_products",
    )(in_smem(table), moved, adjacency)


def near_products(table, group, adjacency, own):
    tiles, padded, _ = own.shape
    count = group.shape[0]

    def kernel(t_ref, group_ref, a_ref, own_ref, out_ref, s_ref):
        s_ref[0] = jnp.zeros((padded, TILE), BF16)
        for k in range(count):
            s_ref[1 + k] = group_ref[k]
        pair_products(t_ref, 1, s_ref, a_ref, out_ref)
        out_ref[...] += own_ref[...]

    return call(
        kernel,
        shape((tiles, padded, TILE), F32),
        [SMEM, VMEM, VMEM, VMEM],
        [pltpu.VMEM((1 + count, padded, TILE), BF16)],
        name="near_products",
    )(in_smem(table), group, adjacency, own)


def hop(table, boundary, adjacency, own, start, exports, last):
    tiles, padded, _ = start.shape
    count = len(boundary)
    sources = sum(b.shape[0] for b in boundary)

    def kernel(*refs):
        t_ref = refs[0]
        boundary_refs = refs[1 : 1 + count]
        a_ref, own_ref, start_ref, export_ref, first_out, second_out, s_ref, acc_ref = refs[1 + count :]
        s_ref[0] = jnp.zeros((padded, TILE), BF16)
        at = 1
        for ref in boundary_refs:
            for k in range(ref.shape[0]):
                s_ref[at] = ref[k]
                at += 1
        pair_products(t_ref, 2, s_ref, a_ref, acc_ref)
        moved_out = []
        for i in range(tiles):
            spread = own_ref[i] + acc_ref[i]
            residual = (1.0 - alpha_mix) * start_ref[i] + alpha_mix * spread
            if last:
                first_out[i] = residual
                second_out[i : i + 1, :] = jnp.sum(residual * residual, axis=0, keepdims=True)
            else:
                moved_out.append(residual.astype(BF16))
                first_out[i] = moved_out[-1]
        if not last:
            second_out[...] = exported_columns(moved_out, export_ref[...])

    if last:
        outs = [shape((tiles, padded, TILE), F32), shape((tiles, TILE), F32)]
    else:
        outs = [shape((tiles, padded, TILE), BF16), shape((padded, TILE), BF16)]
    return call(
        kernel,
        outs,
        [SMEM] + [VMEM] * (count + 4),
        [pltpu.VMEM((1 + sources, padded, TILE), BF16), pltpu.VMEM((tiles, padded, TILE), F32)],
        name="hop",
    )(in_smem(table), *boundary, adjacency, own, start, exports)


def blend_terms(base, residual, labels, mask, gain, ids):
    tiles, padded, _ = base.shape

    def kernel(ids_ref, base_ref, residual_ref, label_ref, mask_ref, gain_ref, term_ref, factor_ref):
        ids = ids_ref[...]
        gains = gain_ref[...]
        for i in range(tiles):
            truth = jnp.where(ids == label_ref[i : i + 1, :], 1.0, 0.0)
            trained = mask_ref[i : i + 1, :] == 1
            term_ref[i] = jnp.where(trained, truth, base_ref[i])
            factor_ref[i] = jnp.where(trained, 0.0, gains * residual_ref[i])

    full = shape((tiles, padded, TILE), F32)
    return call(kernel, [full, full], [VMEM] * 6, name="blend_terms")(
        ids, base, residual, labels, mask, gain
    )


def blend(term, factor, squares, classes, class_total):
    tiles, padded, _ = term.shape
    count = len(squares)
    cuts = 4
    each = tiles // cuts

    def kernel(term_ref, factor_ref, *refs):
        square_refs = refs[:count]
        out_hbm, out_ref, sems = refs[count:]
        total = square_refs[0][...]
        for other in square_refs[1:]:
            total = total + other[...]
        inverse = lax.rsqrt(total / float(class_total) + spread_eps)
        copies = []
        for cut in range(cuts):
            for i in range(cut * each, (cut + 1) * each):
                blended = term_ref[i] + factor_ref[i] * inverse[i : i + 1, :]
                out_ref[:, i * TILE : (i + 1) * TILE] = blended[:classes]
            cols = pl.ds(cut * each * TILE, each * TILE)
            copy = pltpu.make_async_copy(out_ref.at[:, cols], out_hbm.at[:, cols], sems.at[cut])
            copy.start()
            copies.append(copy)
        for copy in copies:
            copy.wait()

    return call(
        kernel,
        shape((classes, tiles * TILE), F32),
        [VMEM] * (count + 2),
        [pltpu.VMEM((classes, tiles * TILE), F32), pltpu.SemaphoreType.DMA((cuts,))],
        name="blend",
        where=HBM,
    )(term, factor, *squares)


def exchanged(value, axis, count, step):
    return lax.ppermute(value, axis, [(i, step_between(i, step, count)) for i in range(count)])


def from_all(value, axis):
    count = lax.axis_size(axis)
    steps = sorted(range(1, count), key=lambda step: (step + 1) % 4 if axis == "node" else step)
    got = {step: exchanged(value, axis, count, step) for step in steps}
    return [value] + [got[step] for step in range(1, count)]


def shards(
    features,
    class_weight,
    class_bias,
    part_position,
    labels,
    train_mask,
    export_rows,
    tile_coords,
    tile_count,
    adjacency,
    corr_gain,
):
    node_count = lax.axis_size("node")
    row_count = lax.axis_size("row")
    part_count = node_count * row_count
    rows_here = part_position.shape[0]
    classes = class_bias.shape[0]
    class_total = classes * lax.axis_size("cls")
    padded = up(classes + 1, 16)
    tiles = rows_here // TILE
    capacity = 2 * rows_here // part_count
    counts = (node_count, row_count)
    labels = labels.reshape(tiles, TILE)
    mask = train_mask.reshape(tiles, TILE)
    weight = class_weight.T
    share = capacity // LO
    direct = share == TILE
    parts = partial_scores(features, weight, row_count, rows_here, padded)
    partials = [
        exchanged(parts[step - 1], "row", row_count, step) for step in range(1, row_count)
    ]
    rest = (labels, mask, export_rows, class_bias[None], corr_gain[None], adjacency[0])
    score, aux, hot, table, labels, mask, exports, bias, gain, adjacency, ids = own_tables(
        features,
        weight,
        part_position.reshape(tiles, TILE),
        tile_coords[0],
        tile_count,
        rest,
        counts,
        padded,
        capacity,
        direct,
    )
    sending = compact_scores([score] + partials, bias, aux, hot, classes, padded)
    if direct:
        axes = ("node", "row")
        received = [sending[0]] + [
            exchanged(sending[step], axes, part_count, step) for step in ([2, 7, 6, 5, 4, 3, 1] if part_count == 8 else range(1, part_count))
        ]
    else:
        blocks, width = len(sending), sending[0].shape[0]
        sent = jnp.stack(sending)
        sent = sent.reshape(blocks, width, TILE // share, share).transpose(0, 2, 1, 3)
        sent = sent.reshape(part_count, width, share)
        got = lax.all_to_all(sent, ("node", "row"), split_axis=0, concat_axis=0, tiled=True)
        got = got.reshape(blocks, TILE // share, width, share).transpose(0, 2, 1, 3)
        got = got.reshape(blocks, width, TILE)
        received = [got[s] for s in range(blocks)]
    first = place_first(received[:FIRST], rows_here, classes, padded)
    raised, total = place_scores(first, received[FIRST:], rows_here, classes, padded)
    totals = from_all(total, "cls")
    moved, out, total = first_moved(raised, totals, labels, mask, exports, ids)
    base, start = start_residuals(raised, total, labels, mask, ids)
    for index in range(HOPS):
        group = jnp.stack(from_all(out, "row"))
        own = own_products(table, moved, adjacency)
        group, own = lax.optimization_barrier((group, own))
        _, *boundary = from_all(group, "node")
        own = near_products(table, group, adjacency, own)
        moved, out = hop(
            table, boundary, adjacency, own, start, exports, index == HOPS - 1
        )
    squares = from_all(out, "cls")
    term, factor = blend_terms(base, moved, labels, mask, gain, ids)
    return blend(term, factor, squares, classes, class_total)


def solution(mesh):
    in_specs = (
        P("row", "node"),
        P("row", "cls"),
        P("cls"),
        P(("node", "row")),
        P(("node", "row")),
        P(("node", "row")),
        P(("node", "row"), None),
        P(("node", "row"), None, None),
        P(("node", "row")),
        P(("node", "row"), None, None, None),
        P("cls"),
    )
    out_specs = P("cls", ("node", "row"))
    return jax.shard_map(shards, mesh=mesh, in_specs=in_specs, out_specs=out_specs, check_vma=False)
```

```python
import jax
import jax.numpy as jnp
from jax import lax
from jax.experimental import pallas as pl
from jax.experimental.pallas import tpu as pltpu
from jax.sharding import PartitionSpec as P

HOPS = 2
TILE = 128
LO = 4
GROUP = 16
REST = 4
FIRST = 5

alpha_mix = 0.8
spread_eps = 1e-06

F32 = jnp.float32
BF16 = jnp.bfloat16
I32 = jnp.int32
VMEM = pl.BlockSpec(memory_space=pltpu.VMEM)
HBM = pl.BlockSpec(memory_space=pltpu.HBM)
SMEM = pl.BlockSpec(memory_space=pltpu.SMEM)


def iota(shape, dim):
    return lax.broadcasted_iota(I32, shape, dim)


def call(kernel, outs, ins, scratch=(), mb=12, flops=0, nbytes=0, name=None, where=None):
    return pl.pallas_call(
        kernel,
        out_shape=outs,
        in_specs=ins,
        out_specs=where or jax.tree.map(lambda _: VMEM, outs),
        scratch_shapes=list(scratch),
        compiler_params=pltpu.CompilerParams(vmem_limit_bytes=mb << 20),
        cost_estimate=pl.CostEstimate(flops=flops, bytes_accessed=nbytes, transcendentals=0),
        name=name,
    )


def in_hbm(*arrays):
    return [pltpu.with_memory_space_constraint(x, pltpu.HBM) for x in arrays]


def in_smem(x):
    return pltpu.with_memory_space_constraint(x, pltpu.SMEM)


def shape(dims, dtype):
    return jax.ShapeDtypeStruct(dims, dtype)


def up(value, step):
    return -(-value // step) * step


def step_between(a, b, count):
    assert count & (count - 1) == 0
    return a ^ b


def padded_weight(weight, padded):
    classes, depth = weight.shape
    weight = weight.astype(F32)
    return jnp.concatenate([weight, jnp.zeros((padded - classes, depth), F32)], axis=0).astype(BF16)


def node_block(ref, step, row_count, rows_here):
    at = step_between(lax.axis_index("row").astype(I32), step, row_count) * rows_here
    return ref.at[:, pl.ds(pl.multiple_of(at, TILE), rows_here)]


def partial_scores(features, weight, row_count, rows_here, padded):
    classes, depth = weight.shape
    steps = range(1, row_count)

    def kernel(f_hbm, w_hbm, *refs):
        outs = refs[: row_count - 1]
        f_ref, w_ref, sems = refs[row_count - 1 :]
        copies = [pltpu.make_async_copy(w_hbm, w_ref, sems.at[0])]
        for step in steps:
            source = node_block(f_hbm, step, row_count, rows_here)
            copies.append(pltpu.make_async_copy(source, f_ref.at[step - 1], sems.at[step]))
        for copy in copies:
            copy.start()
        copies[0].wait()
        w = padded_weight(w_ref[...], padded)
        for step in steps:
            copies[step].wait()
            score = jnp.dot(w, f_ref[step - 1], preferred_element_type=F32)
            outs[step - 1][...] = score.astype(BF16)

    out = shape((padded, rows_here), BF16)
    scratch = [
        pltpu.VMEM((row_count - 1, depth, rows_here), BF16),
        pltpu.VMEM((classes, depth), BF16),
        pltpu.SemaphoreType.DMA((row_count,)),
    ]
    return call(
        kernel, [out] * (row_count - 1), [HBM, HBM], scratch, name="partial_scores"
    )(*in_hbm(features, weight))


def slot_tables(pos, me, rows_here, part_count, capacity, aux_ref, hot_ref):
    tiles = rows_here // TILE
    share = capacity // LO
    columns = part_count * share
    block = pos // rows_here
    before = (iota((TILE, TILE), 0) < iota((TILE, TILE), 1)).astype(BF16)
    ones = jnp.ones((TILE, TILE), BF16)
    above = (iota((tiles, tiles), 1) < iota((tiles, tiles), 0)).astype(BF16)
    rank = jnp.zeros((tiles, TILE), F32)
    for d in range(part_count):
        member = block == d
        m = member.astype(F32).astype(BF16)
        inside = jnp.dot(m, before, preferred_element_type=F32)
        each = jnp.dot(m, ones, preferred_element_type=F32).astype(BF16)
        offset = jnp.dot(above, each, preferred_element_type=F32)
        rank = jnp.where(member, inside + offset, rank)
    rank = rank.astype(I32)
    low = rank // share
    column = step_between(block, me, part_count) * share + (rank - low * share)
    place = pos - block * rows_here
    power = place // TILE
    scale = jnp.ones((tiles, TILE), F32)
    for j in range(1, tiles):
        scale = jnp.where(power >= j, 2.0 * scale, scale)
    aux_ref[0] = low.astype(F32)
    aux_ref[1] = (place - power * TILE + TILE).astype(F32) * scale
    turned = jnp.concatenate([column, jnp.zeros((TILE - tiles, TILE), I32)], axis=0)
    turned = turned.astype(F32).T.astype(I32)
    across = iota((TILE, columns), 1)
    for j in range(tiles):
        hot = jnp.where(across == turned[:, j : j + 1], 1.0, 0.0)
        hot_ref[j * TILE : (j + 1) * TILE, :] = hot.astype(BF16)


def pair_tables(coords, live, here, counts, row_tiles, table_ref):
    node_count, row_count = counts
    slots = coords.shape[1]
    places = up(slots + row_tiles, 2 * REST)
    row = coords[0:1, :]
    column = coords[1:2, :]
    slot = iota((1, slots), 1)
    part = jnp.maximum(column - row_tiles, 0)
    part_node = part // row_count
    part_row = part - part_node * row_count
    node_step = step_between(part_node, here[0], node_count)
    row_step = step_between(part_row, here[1], row_count)
    before = (iota((slots, slots), 0) < iota((slots, slots), 1)).astype(BF16)
    ones = jnp.ones((slots, slots), BF16)
    above = (iota((row_tiles, row_tiles), 1) < iota((row_tiles, row_tiles), 0)).astype(BF16)
    line = iota((8, slots), 0)
    lane = iota((8, places), 1)
    for kind in range(3):
        if kind == 0:
            source = column
            wanted = column < row_tiles
        elif kind == 1:
            source = row_step
            wanted = (column >= row_tiles) & (node_step == 0)
        else:
            source = (node_step - 1) * row_count + row_step
            wanted = (column >= row_tiles) & (node_step > 0)
        member = (iota((row_tiles, slots), 0) == row) & (slot < live) & wanted
        m = jnp.where(member, 1.0, 0.0).astype(BF16)
        rank = jnp.dot(m, before, preferred_element_type=F32)
        number = jnp.dot(m, ones, preferred_element_type=F32).astype(I32)
        pairs = ((number + 1) // 2).astype(F32)
        first = jnp.dot(above, pairs.astype(BF16), preferred_element_type=F32)
        place = jnp.sum(jnp.where(member, 2.0 * first + rank + 1.0, 0.0), axis=0, keepdims=True)
        place = place.astype(I32) - 1
        hot = jnp.where(iota((places, slots), 0) == place, 1.0, 0.0).astype(BF16)
        values = jnp.where(
            line == 0, slot, jnp.where(line == 1, source + 1, jnp.where(line == 2, row, 0))
        )
        table = lax.dot_general(
            values.astype(F32).astype(BF16), hot, (((1,), (1,)), ((), ())), preferred_element_type=F32
        )
        total = jnp.sum(pairs, axis=0, keepdims=True).astype(I32)[:, :1]
        groups = total // GROUP
        rest = (total - groups * GROUP + REST - 1) // REST
        sizes = jnp.where(lane == 0, groups, rest)
        table_ref[kind] = jnp.where(iota((8, places), 0) == 3, sizes, table.astype(I32))


def own_tables(features, weight, positions, coords, live, rest, counts, padded, capacity, direct):
    node_count, row_count = counts
    classes, depth = weight.shape
    tiles = positions.shape[0]
    rows_here = tiles * TILE
    part_count = node_count * row_count
    columns = part_count * capacity // LO
    labels, mask, exports, bias, gain, adjacency = rest
    slots = adjacency.shape[0]

    def kernel(live_ref, *refs):
        node, row = lax.axis_index("node").astype(I32), lax.axis_index("row").astype(I32)
        f_hbm, w_hbm, p_hbm, c_hbm, l_hbm, m_hbm, e_hbm, b_hbm, g_hbm, a_hbm = refs[:10]
        score_ref, aux_ref, hot_ref, table_out, l_ref, m_ref, e_out, b_out, g_out, a_ref, i_out = refs[10:21]
        f_ref, w_ref, p_ref, c_ref, b_ref, g_ref, t_ref, e_ref, sems = refs[21:]
        source = node_block(f_hbm, 0, row_count, rows_here)
        pairs = [
            (p_hbm, p_ref),
            (c_hbm, c_ref),
            (b_hbm, b_ref),
            (g_hbm, g_ref),
            (e_hbm, e_ref),
            (w_hbm, w_ref),
            (source, f_ref),
            (l_hbm, l_ref),
            (m_hbm, m_ref),
            (a_hbm, a_ref),
        ]
        copies = [pltpu.make_async_copy(a, b, sems.at[i]) for i, (a, b) in enumerate(pairs)]
        for copy in copies:
            copy.start()
        for copy in copies[:5]:
            copy.wait()
        me = node * row_count + row if direct else 0
        slot_tables(p_ref[...], me, rows_here, part_count, capacity, aux_ref, hot_ref)
        pair_tables(c_ref[...], live_ref[0], (node, row), counts, tiles, t_ref)
        table_copy = pltpu.make_async_copy(t_ref, table_out, sems.at[10])
        table_copy.start()
        b_out[...] = jnp.broadcast_to(turned_column(b_ref[...], padded), (padded, TILE))
        g_out[...] = jnp.broadcast_to(turned_column(g_ref[...], padded), (padded, TILE))
        chosen = iota((rows_here, TILE), 0) == e_ref[...]
        e_out[...] = jnp.where(chosen, 1.0, 0.0).astype(BF16)
        line = iota((padded, TILE), 0)
        first = lax.axis_index("cls").astype(I32) * classes
        i_out[...] = jnp.where(line < classes, line + first, -1)
        table_copy.wait()
        for copy in copies[5:]:
            copy.wait()
        w = padded_weight(w_ref[...], padded)
        score_ref[...] = jnp.dot(w, f_ref[...], preferred_element_type=F32).astype(BF16)

    like = [shape(x.shape, x.dtype) for x in rest]
    outs = [
        shape((padded, rows_here), BF16),
        shape((2, tiles, TILE), F32),
        shape((rows_here, columns), BF16),
        pltpu.SMEM((3, 8, up(slots + tiles, 2 * REST)), I32),
        like[0],
        like[1],
        shape((rows_here, TILE), BF16),
        shape((padded, TILE), F32),
        shape((padded, TILE), F32),
        like[5],
        shape((padded, TILE), I32),
    ]
    scratch = [
        pltpu.VMEM((depth, rows_here), BF16),
        pltpu.VMEM((classes, depth), BF16),
        pltpu.VMEM(positions.shape, I32),
        pltpu.VMEM(coords.shape, I32),
        pltpu.VMEM(bias.shape, F32),
        pltpu.VMEM(gain.shape, F32),
        pltpu.VMEM(outs[3].shape, I32),
        pltpu.VMEM(exports.shape, I32),
        pltpu.SemaphoreType.DMA((11,)),
    ]
    where = [VMEM] * 3 + [SMEM] + [VMEM] * 7
    return call(kernel, outs, [SMEM] + [HBM] * 10, scratch, name="own_tables", where=where)(
        live, *in_hbm(features, weight, positions, coords, *rest)
    )


def turned_column(row, padded):
    row = jnp.concatenate([row, jnp.zeros((1, TILE - row.shape[1]), F32)], axis=1)
    return jnp.broadcast_to(row, (8, TILE)).T[:padded, 0:1]


def laid_block(laid, at, rows, padded):
    block = laid[:, at * TILE : (at + 1) * TILE]
    kept = jnp.concatenate([block[l * padded : l * padded + rows] for l in range(LO)], axis=0)
    return kept.astype(BF16)


def compact_scores(partials, bias, aux, hot, classes, padded):
    count = len(partials)
    rows_here = partials[0].shape[1]
    tiles = rows_here // TILE
    rows = classes + 1

    def kernel(*refs):
        parts = refs[:count]
        b_ref, aux_ref, hot_ref = refs[count : count + 3]
        outs, x_ref = refs[count + 3 : -1], refs[-1]
        bias_column = b_ref[...]
        row = iota((padded, TILE), 0)
        for j in range(tiles):
            cols = slice(j * TILE, (j + 1) * TILE)
            total = parts[0][:, cols].astype(F32)
            for other in parts[1:]:
                total = total + other[:, cols].astype(F32)
            value = (total + bias_column).astype(BF16).astype(F32)
            low = aux_ref[0, j : j + 1, :]
            value = jnp.where(row == classes, aux_ref[1, j : j + 1, :], value)
            for l in range(LO):
                x_ref[l * padded : (l + 1) * padded, cols] = jnp.where(low == l, value, 0.0).astype(BF16)
        laid = jnp.dot(x_ref[...], hot_ref[...], preferred_element_type=F32)
        for d, out in enumerate(outs):
            out[...] = laid_block(laid, d, rows, padded)

    return call(
        kernel,
        [shape((LO * rows, TILE), BF16)] * (hot.shape[1] // TILE),
        [VMEM] * (count + 3),
        [pltpu.VMEM((LO * padded, rows_here), BF16)],
        name="compact_scores",
    )(*partials, bias, aux, hot)


def placed(r_refs, x_ref, hot_ref, rows_here, classes, padded):
    rows = classes + 1
    high = rows_here // LO
    blocks = len(r_refs)
    width = LO * rows
    pick = iota((8, width), 1) - iota((8, width), 0) * rows == classes
    pick = jnp.where(pick & (iota((8, width), 0) < LO), 1.0, 0.0).astype(BF16)
    held = [jnp.dot(pick, ref[...], preferred_element_type=F32) for ref in r_refs]
    held = jnp.concatenate(held, axis=0)
    power = jnp.zeros(held.shape, I32)
    scale = jnp.ones(held.shape, F32)
    for j in range(1, rows_here // TILE):
        above = held >= float(TILE << j)
        power = jnp.where(above, j, power)
        scale = jnp.where(above, 0.5**j, scale)
    code = jnp.where(held > 0.0, power * TILE + (held * scale).astype(I32) - TILE, -1)
    group = jnp.where(code < 0, -1, code // high)
    inner = (code & (high - 1)).astype(F32)
    rest = jnp.zeros((TILE - 8 * blocks, TILE), F32)
    turned = jnp.concatenate([inner, rest], axis=0).T.astype(I32)
    across = iota((TILE, high), 1)
    tail = jnp.zeros((padded - rows, TILE), F32)
    for s in range(blocks):
        block = r_refs[s][...].astype(F32)
        for l in range(LO):
            at = (s * LO + l) * TILE
            lane = s * 8 + l
            hot = jnp.where(across == turned[:, lane : lane + 1], 1.0, 0.0)
            hot_ref[at : at + TILE, :] = hot.astype(BF16)
            value = jnp.concatenate([block[l * rows : (l + 1) * rows], tail], axis=0)
            mine = group[lane : lane + 1, :]
            for q in range(LO):
                x_ref[q * padded : (q + 1) * padded, at : at + TILE] = jnp.where(
                    mine == q, value, 0.0
                ).astype(BF16)
    return jnp.dot(x_ref[...], hot_ref[...], preferred_element_type=F32)


def place_scratch(blocks, rows_here, padded):
    width = blocks * LO * TILE
    return [pltpu.VMEM((LO * padded, width), BF16), pltpu.VMEM((width, rows_here // LO), BF16)]


def place_first(received, rows_here, classes, padded):
    blocks = len(received)

    def kernel(*refs):
        out_ref, x_ref, hot_ref = refs[blocks:]
        out_ref[...] = placed(refs[:blocks], x_ref, hot_ref, rows_here, classes, padded)

    flops = 2 * LO * padded * rows_here * blocks * TILE
    return call(
        kernel,
        [shape((LO * padded, rows_here // LO), F32)],
        [VMEM] * blocks,
        place_scratch(blocks, rows_here, padded),
        flops=flops,
        nbytes=4 * LO * padded * rows_here // LO,
        name="place_first",
    )(*received)[0]


def place_scores(first, received, rows_here, classes, padded):
    blocks = len(received)
    tiles = rows_here // TILE

    def kernel(*refs):
        first_ref = refs[0]
        raised_ref, total_ref, x_ref, hot_ref = refs[1 + blocks :]
        logits = placed(refs[1 : 1 + blocks], x_ref, hot_ref, rows_here, classes, padded)
        logits = logits + first_ref[...]
        row = iota((padded, TILE), 0)
        for i in range(tiles):
            q, c = divmod(i, tiles // LO)
            part = logits[q * padded : (q + 1) * padded, c * TILE : (c + 1) * TILE]
            raised = jnp.where(row < classes, jnp.exp(part), 0.0)
            raised_ref[i] = raised
            total_ref[i : i + 1, :] = jnp.sum(raised, axis=0, keepdims=True)

    return call(
        kernel,
        [shape((tiles, padded, TILE), F32), shape((tiles, TILE), F32)],
        [VMEM] * (1 + blocks),
        place_scratch(blocks, rows_here, padded),
        name="place_scores",
    )(first, *received)


def exported_columns(moved_tiles, chosen):
    source = jnp.concatenate(moved_tiles, axis=1)
    return jnp.dot(source, chosen, preferred_element_type=F32).astype(BF16)


def start_residuals(raised, totals, labels, mask, exports, ids):
    tiles, padded, _ = raised.shape
    count = len(totals)

    def kernel(ids_ref, raised_ref, *refs):
        total_refs = refs[:count]
        label_ref, mask_ref, export_ref, base_ref, start_ref, moved_ref, out_ref = refs[count:]
        total = total_refs[0][...]
        for other in total_refs[1:]:
            total = total + other[...]
        ids = ids_ref[...]
        moved = []
        for i in range(tiles):
            base = raised_ref[i] / total[i : i + 1, :]
            truth = jnp.where(ids == label_ref[i : i + 1, :], 1.0, 0.0)
            start = mask_ref[i : i + 1, :].astype(F32) * (truth - base)
            base_ref[i] = base
            start_ref[i] = start
            moved.append(start.astype(BF16))
            moved_ref[i] = moved[-1]
        out_ref[...] = exported_columns(moved, export_ref[...])

    full = shape((tiles, padded, TILE), F32)
    outs = [full, full, shape((tiles, padded, TILE), BF16), shape((padded, TILE), BF16)]
    return call(kernel, outs, [VMEM] * (count + 5), name="start_residuals")(
        ids, raised, *totals, labels, mask, exports
    )


def pair_products(table_ref, kind, s_ref, a_ref, acc_ref):
    acc_ref[...] = jnp.zeros_like(acc_ref)

    def product(k):
        slots = [table_ref[kind, 0, k], table_ref[kind, 0, k + 1]]
        sources = [table_ref[kind, 1, k], table_ref[kind, 1, k + 1]]
        left = jnp.concatenate([s_ref[j] for j in sources], axis=1)
        right = jnp.concatenate([a_ref[t] for t in slots], axis=1)
        acc_ref[table_ref[kind, 2, k]] += lax.dot_general(
            left, right, (((1,), (1,)), ((), ())), preferred_element_type=F32
        )

    def several(first, count):
        def step(group, carry):
            for u in range(count):
                product(2 * (first + group * count + u))
            return carry

        return step

    groups = table_ref[kind, 3, 0]
    lax.fori_loop(0, groups, several(0, GROUP), 0)
    lax.fori_loop(0, table_ref[kind, 3, 1], several(groups * GROUP, REST), 0)


def own_products(table, moved, adjacency):
    tiles, padded, _ = moved.shape

    def kernel(t_ref, moved_ref, a_ref, acc_ref, s_ref):
        s_ref[0] = jnp.zeros((padded, TILE), BF16)
        for i in range(tiles):
            s_ref[1 + i] = moved_ref[i]
        pair_products(t_ref, 0, s_ref, a_ref, acc_ref)

    return call(
        kernel,
        shape((tiles, padded, TILE), F32),
        [SMEM, VMEM, VMEM],
        [pltpu.VMEM((1 + tiles, padded, TILE), BF16)],
        name="own_products",
    )(in_smem(table), moved, adjacency)


def near_products(table, group, adjacency, own):
    tiles, padded, _ = own.shape
    count = group.shape[0]

    def kernel(t_ref, group_ref, a_ref, own_ref, out_ref, s_ref):
        s_ref[0] = jnp.zeros((padded, TILE), BF16)
        for k in range(count):
            s_ref[1 + k] = group_ref[k]
        pair_products(t_ref, 1, s_ref, a_ref, out_ref)
        out_ref[...] += own_ref[...]

    return call(
        kernel,
        shape((tiles, padded, TILE), F32),
        [SMEM, VMEM, VMEM, VMEM],
        [pltpu.VMEM((1 + count, padded, TILE), BF16)],
        name="near_products",
    )(in_smem(table), group, adjacency, own)


def hop(table, boundary, adjacency, own, start, exports, last):
    tiles, padded, _ = start.shape
    count = len(boundary)
    sources = sum(b.shape[0] for b in boundary)

    def kernel(*refs):
        t_ref = refs[0]
        boundary_refs = refs[1 : 1 + count]
        a_ref, own_ref, start_ref, export_ref, first_out, second_out, s_ref, acc_ref = refs[1 + count :]
        s_ref[0] = jnp.zeros((padded, TILE), BF16)
        at = 1
        for ref in boundary_refs:
            for k in range(ref.shape[0]):
                s_ref[at] = ref[k]
                at += 1
        pair_products(t_ref, 2, s_ref, a_ref, acc_ref)
        moved_out = []
        for i in range(tiles):
            spread = own_ref[i] + acc_ref[i]
            residual = (1.0 - alpha_mix) * start_ref[i] + alpha_mix * spread
            if last:
                first_out[i] = residual
                second_out[i : i + 1, :] = jnp.sum(residual * residual, axis=0, keepdims=True)
            else:
                moved_out.append(residual.astype(BF16))
                first_out[i] = moved_out[-1]
        if not last:
            second_out[...] = exported_columns(moved_out, export_ref[...])

    if last:
        outs = [shape((tiles, padded, TILE), F32), shape((tiles, TILE), F32)]
    else:
        outs = [shape((tiles, padded, TILE), BF16), shape((padded, TILE), BF16)]
    return call(
        kernel,
        outs,
        [SMEM] + [VMEM] * (count + 4),
        [pltpu.VMEM((1 + sources, padded, TILE), BF16), pltpu.VMEM((tiles, padded, TILE), F32)],
        name="hop",
    )(in_smem(table), *boundary, adjacency, own, start, exports)


def blend_terms(base, residual, labels, mask, gain, ids):
    tiles, padded, _ = base.shape

    def kernel(ids_ref, base_ref, residual_ref, label_ref, mask_ref, gain_ref, term_ref, factor_ref):
        ids = ids_ref[...]
        gains = gain_ref[...]
        for i in range(tiles):
            truth = jnp.where(ids == label_ref[i : i + 1, :], 1.0, 0.0)
            trained = mask_ref[i : i + 1, :] == 1
            term_ref[i] = jnp.where(trained, truth, base_ref[i])
            factor_ref[i] = jnp.where(trained, 0.0, gains * residual_ref[i])

    full = shape((tiles, padded, TILE), F32)
    return call(kernel, [full, full], [VMEM] * 6, name="blend_terms")(
        ids, base, residual, labels, mask, gain
    )


def blend(term, factor, squares, classes, class_total):
    tiles, padded, _ = term.shape
    count = len(squares)
    cuts = 2
    each = tiles // cuts

    def kernel(term_ref, factor_ref, *refs):
        square_refs = refs[:count]
        out_hbm, out_ref, sems = refs[count:]
        total = square_refs[0][...]
        for other in square_refs[1:]:
            total = total + other[...]
        inverse = lax.rsqrt(total / float(class_total) + spread_eps)
        copies = []
        for cut in range(cuts):
            for i in range(cut * each, (cut + 1) * each):
                blended = term_ref[i] + factor_ref[i] * inverse[i : i + 1, :]
                out_ref[:, i * TILE : (i + 1) * TILE] = blended[:classes]
            cols = pl.ds(cut * each * TILE, each * TILE)
            copy = pltpu.make_async_copy(out_ref.at[:, cols], out_hbm.at[:, cols], sems.at[cut])
            copy.start()
            copies.append(copy)
        for copy in copies:
            copy.wait()

    return call(
        kernel,
        shape((classes, tiles * TILE), F32),
        [VMEM] * (count + 2),
        [pltpu.VMEM((classes, tiles * TILE), F32), pltpu.SemaphoreType.DMA((cuts,))],
        name="blend",
        where=HBM,
    )(term, factor, *squares)


def exchanged(value, axis, count, step):
    return lax.ppermute(value, axis, [(i, step_between(i, step, count)) for i in range(count)])


def from_all(value, axis):
    count = lax.axis_size(axis)
    steps = sorted(range(1, count), key=lambda step: (step + 1) % 4 if axis == "node" else step)
    got = {step: exchanged(value, axis, count, step) for step in steps}
    return [value] + [got[step] for step in range(1, count)]


def shards(
    features,
    class_weight,
    class_bias,
    part_position,
    labels,
    train_mask,
    export_rows,
    tile_coords,
    tile_count,
    adjacency,
    corr_gain,
):
    node_count = lax.axis_size("node")
    row_count = lax.axis_size("row")
    part_count = node_count * row_count
    rows_here = part_position.shape[0]
    classes = class_bias.shape[0]
    class_total = classes * lax.axis_size("cls")
    padded = up(classes + 1, 16)
    tiles = rows_here // TILE
    capacity = 2 * rows_here // part_count
    counts = (node_count, row_count)
    labels = labels.reshape(tiles, TILE)
    mask = train_mask.reshape(tiles, TILE)
    weight = class_weight.T
    share = capacity // LO
    direct = share == TILE
    parts = partial_scores(features, weight, row_count, rows_here, padded)
    partials = [
        exchanged(parts[step - 1], "row", row_count, step) for step in range(1, row_count)
    ]
    rest = (labels, mask, export_rows, class_bias[None], corr_gain[None], adjacency[0])
    score, aux, hot, table, labels, mask, exports, bias, gain, adjacency, ids = own_tables(
        features,
        weight,
        part_position.reshape(tiles, TILE),
        tile_coords[0],
        tile_count,
        rest,
        counts,
        padded,
        capacity,
        direct,
    )
    sending = compact_scores([score] + partials, bias, aux, hot, classes, padded)
    if direct:
        axes = ("node", "row")
        received = [sending[0]] + [
            exchanged(sending[step], axes, part_count, step) for step in ([2, 7, 6, 5, 4, 3, 1] if part_count == 8 else range(1, part_count))
        ]
    else:
        blocks, width = len(sending), sending[0].shape[0]
        sent = jnp.stack(sending)
        sent = sent.reshape(blocks, width, TILE // share, share).transpose(0, 2, 1, 3)
        sent = sent.reshape(part_count, width, share)
        got = lax.all_to_all(sent, ("node", "row"), split_axis=0, concat_axis=0, tiled=True)
        got = got.reshape(blocks, TILE // share, width, share).transpose(0, 2, 1, 3)
        got = got.reshape(blocks, width, TILE)
        received = [got[s] for s in range(blocks)]
    first = place_first(received[:FIRST], rows_here, classes, padded)
    raised, total = place_scores(first, received[FIRST:], rows_here, classes, padded)
    totals = from_all(total, "cls")
    base, start, moved, out = start_residuals(
        raised, totals, labels, mask, exports, ids
    )
    for index in range(HOPS):
        group = jnp.stack(from_all(out, "row"))
        own = own_products(table, moved, adjacency)
        group, own = lax.optimization_barrier((group, own))
        _, *boundary = from_all(group, "node")
        own = near_products(table, group, adjacency, own)
        moved, out = hop(
            table, boundary, adjacency, own, start, exports, index == HOPS - 1
        )
    squares = from_all(out, "cls")
    term, factor = blend_terms(base, moved, labels, mask, gain, ids)
    return blend(term, factor, squares, classes, class_total)


def solution(mesh):
    in_specs = (
        P("row", "node"),
        P("row", "cls"),
        P("cls"),
        P(("node", "row")),
        P(("node", "row")),
        P(("node", "row")),
        P(("node", "row"), None),
        P(("node", "row"), None, None),
        P(("node", "row")),
        P(("node", "row"), None, None, None),
        P("cls"),
    )
    out_specs = P("cls", ("node", "row"))
    return jax.shard_map(shards, mesh=mesh, in_specs=in_specs, out_specs=out_specs, check_vma=False)
```
